256 devices in a mesh: dp: 16 (over x, y_lo, core), loop: 16 (over y_hi, z).
Axes of the slice: x: 4, y: 4 (y_hi: 2, y_lo: 2; y = y_hi * 2 + y_lo), z: 8, core: 2. Of those that a mesh axis runs over, the one named last changes fastest.
Arguments:
- tokens: bfloat16 [6144, 4096], P('dp')
- cotangent: bfloat16 [6144, 4096], P('dp'), may hold values from -6 to 6
- proj_weight: bfloat16 [4096, 4096], P(None, 'dp')
- rotation: float32 [4096, 4096], P('dp', 'loop')
- doc_lengths: int32 [96], P('dp'), may hold values from 1 to 64, as said below
Outputs:
- riemannian: float32 [4096, 4096], P('dp', 'loop')
The draws below stay inside these ranges and needn't reach their ends.
Inputs may be any that keep to these rules, and one draw needn't show every extreme that they name: `doc_lengths`: each slot holds 1 to 64 tokens; some slot holds exactly 64 in every draw.
All inputs are finite; a program needn't handle non-finite values.
Results may differ from the reference program's by a relative error of at most 0.009.
The reference program's roundings to bfloat16 on the way (of `masked`, `rot_half`, `acts_q`, `mixed_q`, `grad_acts` and `grad_mixed`) count: a program that leaves them out, or rounds other values in their place, can miss the bound.
Values may be sent and summed in bfloat16 or wider, within the bound.
A program may use at most 64 MiB of HBM per device.

```python
import math
import jax
import jax.numpy as jnp
from jax import lax

D = 4096
E = 4096
SLOT = 64
TOKENS = 6144


def draw_tokens(key, part):
    key_values, key_scales = jax.random.split(key, 2)
    row_scales = jnp.exp(jax.random.uniform(key_scales, (TOKENS, 1), jnp.float32, 0.0, math.log(10.0)))
    values = jnp.clip(jax.random.normal(key_values, (TOKENS, D), jnp.float32), -6.0, 6.0)
    return (values * row_scales).astype(jnp.bfloat16)


def draw_proj_weight(key, part):
    key_values, key_scales = jax.random.split(key)
    col_scales = jnp.exp(jax.random.uniform(key_scales, (1, E), jnp.float32, -0.5 * math.log(10.0), 0.5 * math.log(10.0)))
    values = jnp.clip(jax.random.normal(key_values, (D, E), jnp.float32), -6.0, 6.0)
    return (values * col_scales / math.sqrt(D)).astype(jnp.bfloat16)


def draw_rotation(key, part):
    key_rows, key_cols, key_noise = jax.random.split(key, 3)
    row_index = jnp.arange(D, dtype=jnp.int32)[:, None]
    col_index = jnp.arange(D, dtype=jnp.int32)[None, :]
    parity_sum = jnp.zeros((D, D), jnp.int32)
    for bit_place in range(max(D - 1, 1).bit_length()):
        row_bits = jnp.bitwise_and(jnp.right_shift(row_index, bit_place), 1)
        col_bits = jnp.bitwise_and(jnp.right_shift(col_index, bit_place), 1)
        parity_sum = parity_sum + row_bits * col_bits
    parity = parity_sum % 2
    hadamard = 1.0 - 2.0 * parity.astype(jnp.float32)
    row_signs = 1.0 - 2.0 * jax.random.bernoulli(key_rows, 0.5, (D, 1)).astype(jnp.float32)
    col_signs = 1.0 - 2.0 * jax.random.bernoulli(key_cols, 0.5, (1, D)).astype(jnp.float32)
    noise = 0.1 * jnp.clip(jax.random.normal(key_noise, (D, D), jnp.float32), -6.0, 6.0)
    return (row_signs * hadamard * col_signs + noise) / math.sqrt(D)


def draw_doc_lengths(key, part):
    key_lengths, key_pick = jax.random.split(key)
    slot_count = TOKENS // SLOT
    lengths = jax.random.randint(key_lengths, (slot_count,), 1, SLOT + 1, jnp.int32)
    chosen = jax.random.randint(key_pick, (), 0, slot_count, jnp.int32)
    return jnp.where(jnp.arange(slot_count, dtype=jnp.int32) == chosen, SLOT, lengths).astype(jnp.int32)


def block_scale(stream_key, dims, cuts, least, top_value):
    loudness = 1.0
    for axis_at, parts in cuts:
        heights = jax.random.uniform(jax.random.fold_in(jax.random.fold_in(stream_key, 6), axis_at), (parts,), jnp.float32, least / len(cuts), top_value / len(cuts))
        loudness = loudness * jnp.repeat(jnp.exp(heights), dims[axis_at] // parts).reshape((-1,) + (1,) * (len(dims) - 1 - axis_at))
    return loudness


def bell_draw(stream_key, dims, spread, limit, cuts=(), kind=jnp.bfloat16):
    level = block_scale(stream_key, dims, cuts, -0.22, 0.18) if cuts else 1.0
    entries = jax.random.normal(stream_key, dims, jnp.float32) * spread * level
    return jnp.minimum(jnp.maximum(entries, -limit), limit).astype(kind)


def setup_inputs(seed: int = 0) -> dict:
    key_list = jax.random.split(jax.random.key(seed), 6)
    return {
        "tokens": draw_tokens(jax.random.fold_in(key_list[5], 71), 0),
        "cotangent": bell_draw(key_list[1], (TOKENS, E), 1.0, 6.0, ((0, 16),)),
        "proj_weight": draw_proj_weight(jax.random.fold_in(key_list[5], 71), 0),
        "rotation": draw_rotation(jax.random.fold_in(key_list[5], 71), 0),
        "doc_lengths": draw_doc_lengths(jax.random.fold_in(key_list[5], 71), 0),
    }


clip_ratio = 2.0
eps_power = 1e-06

def reference(tokens, cotangent, proj_weight, rotation, doc_lengths):
    positions = jnp.arange(TOKENS, dtype=jnp.int32)
    slot_index = positions // SLOT
    live = positions % SLOT < doc_lengths[slot_index]
    masked = cotangent * live.astype(jnp.bfloat16)[:, None]
    rot_half = rotation.astype(jnp.bfloat16)
    acts = jnp.dot(tokens, rot_half, preferred_element_type=jnp.float32)
    row_limit = clip_ratio * jnp.sqrt(lax.optimization_barrier(jnp.mean(acts * acts, axis=1, keepdims=True)) + eps_power)
    acts_q = jnp.clip(acts, -row_limit, row_limit).astype(jnp.bfloat16)
    mixed = jnp.dot(rot_half.T, proj_weight, preferred_element_type=jnp.float32)
    col_limit = clip_ratio * jnp.sqrt(lax.optimization_barrier(jnp.mean(mixed * mixed, axis=0, keepdims=True)) + eps_power)
    mixed_q = jnp.clip(mixed, -col_limit, col_limit).astype(jnp.bfloat16)
    grad_acts = jnp.dot(masked, mixed_q.T, preferred_element_type=jnp.float32).astype(jnp.bfloat16)
    grad_mixed = jnp.dot(acts_q.T, masked, preferred_element_type=jnp.float32).astype(jnp.bfloat16)
    gradient = jnp.dot(tokens.T, grad_acts, preferred_element_type=jnp.float32)
    gradient = gradient + jnp.dot(proj_weight, grad_mixed.T, preferred_element_type=jnp.float32)
    gradient = gradient * (1.0 / jnp.sqrt(jnp.float32(TOKENS)))
    cross = jnp.dot(gradient.T, rotation, precision=lax.Precision.HIGHEST, preferred_element_type=jnp.float32)
    return gradient - jnp.dot(rotation, cross, precision=lax.Precision.HIGHEST, preferred_element_type=jnp.float32)
```

```python
import jax
import jax.numpy as jnp
from jax import lax
from jax.experimental import pallas as pl
from jax.experimental.pallas import tpu as pltpu
from jax.sharding import PartitionSpec as P

MESH = pl.DeviceIdType.MESH
BF = jnp.bfloat16
F32 = jnp.float32
CLIP_RATIO = 2.0
EPS_POWER = 1e-06
SEMS = 256


def nn(a, b):
    return lax.dot_general(a, b, (((1,), (0,)), ((), ())), preferred_element_type=F32)


def split(v):
    hi = v.astype(BF)
    return hi, (v - hi.astype(F32)).astype(BF)


def drive(*gens):
    live = list(gens)
    while live:
        for g in list(live):
            try:
                next(g)
            except StopIteration:
                live.remove(g)


def kernel(
    inv_width,
    scale,
    len_ref,
    tok_hbm,
    cot_hbm,
    w_hbm,
    rot_hbm,
    out_ref,
    xw,
    xwt,
    cot,
    rhi,
    rlo,
    mqt,
    s32,
    s_hi,
    s_lo,
    stat_mine,
    stat_all,
    gam,
    aqt,
    gat_all,
    gm_all,
    r_all,
    part_a,
    part_b,
    rc,
    rx0,
    rx1,
    ry0,
    ry1,
    ob,
    gout,
    cross,
    ssem,
    rsem,
    lsem,
):
    i = lax.axis_index("dp")
    j = lax.axis_index("loop")
    x, yl, c = i // 4, (i // 2) % 2, i % 2
    yh, z = j // 8, j % 8
    T = tok_hbm.shape[0]
    B = 256
    KB = 16

    def wrap4(v):
        return lax.rem(v + 4, 4)

    def wrap8(v):
        return lax.rem(v + 8, 8)

    xp, xm = wrap4(x + 1), wrap4(x - 1)
    x2 = wrap4(x + 2)
    XP = {"dp": xp * 4 + yl * 2 + c, "loop": j}
    XM = {"dp": xm * 4 + yl * 2 + c, "loop": j}
    YN = {"dp": x * 4 + (1 - yl) * 2 + c, "loop": j}
    CORE = {"dp": x * 4 + yl * 2 + (1 - c), "loop": j}
    zp, zm = wrap8(z + 1), wrap8(z - 1)
    ZP = {"dp": i, "loop": yh * 8 + zp}
    ZM = {"dp": i, "loop": yh * 8 + zm}
    YH = {"dp": i, "loop": (1 - yh) * 8 + z}

    def did(xx, yy, cc):
        return xx * 4 + yy * 2 + cc

    counter = [0]
    sent = []

    def send(src, dst, dev):
        k = counter[0]
        counter[0] += 1
        cp = pltpu.make_async_remote_copy(
            src_ref=src,
            dst_ref=dst,
            send_sem=ssem.at[k],
            recv_sem=rsem.at[k],
            device_id=dev,
            device_id_type=MESH,
        )
        cp.start()
        sent.append(cp)
        return cp

    def send_same(ref, dev):
        return send(ref, ref, dev)

    ld_r = pltpu.make_async_copy(rot_hbm, r_all.at[j], lsem.at[0])
    ld_x = pltpu.make_async_copy(tok_hbm, xw.at[pl.ds(0, T)], lsem.at[1])
    ld_w = pltpu.make_async_copy(w_hbm, xwt.at[:, pl.ds(T, B)], lsem.at[2])
    ld_c = pltpu.make_async_copy(cot_hbm, cot, lsem.at[3])
    ld_r.start()
    ld_w.start()
    ld_x.start()
    ld_c.start()

    barrier = pltpu.get_barrier_semaphore()
    for dev in (XP, XM, YN, CORE):
        pl.semaphore_signal(barrier, inc=1, device_id=dev, device_id_type=MESH)
    for d in range(1, 16):
        pl.semaphore_signal(
            barrier, inc=1, device_id={"dp": i, "loop": lax.rem(j + d, 16)}, device_id_type=MESH
        )
    ld_r.wait()
    rv = r_all[j]
    hv, lv = split(rv)
    own_rows = pl.ds(pl.multiple_of(i * B, B), B)
    rhi[own_rows] = hv
    rlo[own_rows] = lv
    pl.semaphore_wait(barrier, 19)

    def rows(buf, idx, part=None):
        if part is None:
            return buf.at[pl.ds(pl.multiple_of(idx * B, B), B)]
        return buf.at[pl.ds(pl.multiple_of(idx * B + part * (B // 2), B // 2), B // 2)]

    def gather_dp(buf):
        own = rows(buf, i)
        a_y = send_same(own, YN)
        a_p = send_same(own, XP)
        a_m = send_same(own, XM)
        core = [send_same(own, CORE)]
        left, right, opp = did(xm, yl, c), did(xp, yl, c), did(x2, yl, c)
        ynb = did(x, 1 - yl, c)
        yield
        a_p.wait_recv()
        r_p = send_same(rows(buf, left, 0), XP)
        y_l = send_same(rows(buf, left, 1), YN)
        core.append(send_same(rows(buf, left), CORE))
        yield
        a_m.wait_recv()
        r_m = send_same(rows(buf, right, 1), XM)
        y_r = send_same(rows(buf, right, 0), YN)
        core.append(send_same(rows(buf, right), CORE))
        yield
        a_y.wait_recv()
        d_p = send_same(rows(buf, ynb, 0), XP)
        d_m = send_same(rows(buf, ynb, 1), XM)
        core.append(send_same(rows(buf, ynb), CORE))
        yield
        r_p.wait_recv()
        y_a = send_same(rows(buf, opp, 0), YN)
        core.append(send_same(rows(buf, opp, 0), CORE))
        yield
        r_m.wait_recv()
        y_b = send_same(rows(buf, opp, 1), YN)
        core.append(send_same(rows(buf, opp, 1), CORE))
        yield
        lft2, rgt2, opp2 = did(xm, 1 - yl, c), did(xp, 1 - yl, c), did(x2, 1 - yl, c)
        for cp, ref in (
            (d_p, rows(buf, lft2, 0)),
            (d_m, rows(buf, rgt2, 1)),
            (y_l, rows(buf, lft2, 1)),
            (y_r, rows(buf, rgt2, 0)),
            (y_a, rows(buf, opp2, 0)),
            (y_b, rows(buf, opp2, 1)),
        ):
            cp.wait_recv()
            core.append(send_same(ref, CORE))
            yield
        for cp in core:
            cp.wait_recv()

    def gather_loop(buf):
        half = B // 2

        def blk(u, zz, part=None):
            ref = buf.at[u * 8 + zz]
            if part is None:
                return ref
            return ref.at[pl.ds(part * half, half)]

        own = blk(yh, z)
        oth = send_same(own, YH)
        wp = {0: send_same(own, ZP)}
        wm = {0: send_same(own, ZM)}
        lanes = (yh, 1 - yh)
        yield
        oth.wait_recv()
        wp[1] = send_same(blk(lanes[1], z), ZP)
        wm[1] = send_same(blk(lanes[1], z), ZM)
        yield
        for d in range(1, 5):
            for ln in (0, 1):
                wp[ln].wait_recv()
                if d < 4:
                    ref = blk(lanes[ln], wrap8(z - d), None if d < 3 else 0)
                    wp[ln] = send_same(ref, ZP)
                yield
                wm[ln].wait_recv()
                if d < 4:
                    ref = blk(lanes[ln], wrap8(z + d), None if d < 3 else 1)
                    wm[ln] = send_same(ref, ZM)
                yield

    def reduce_dp(k, part, chunk, out):
        rck, r0k, r1k, y0k, y1k, obk = (b.at[k] for b in (rc, rx0, rx1, ry0, ry1, ob))
        order = [(2, 0), (2, 1), (3, 0), (1, 1), (1, 0), (3, 1), (0, 0), (0, 1)]
        half, quar = B // 2, B // 4
        pend = []

        def flush(keep):
            while len(pend) > keep:
                pend.pop(0)()

        core = {}
        for d, yy in order:
            xx = wrap4(x + d)
            idx = did(xx, yy, 1 - c)
            part[idx] = chunk(idx)

            def go(idx=idx, d=d, yy=yy, xx=xx):
                core[d, yy] = send(part.at[idx], rck.at[xx * 2 + yy], CORE)

            pend.append(go)
            flush(1)
            yield
        relay, direct, yfirst = {}, {}, {}
        for d, yy in order:
            xx = wrap4(x + d)
            idx = did(xx, yy, c)
            v = chunk(idx)
            flush(0)
            core[d, yy].wait_recv()
            part[idx] = v + rck[xx * 2 + yy]
            sgn = 1 if yy == 0 else -1
            fwd, back = (XP, XM) if sgn == 1 else (XM, XP)
            if d == 2:

                def go(idx=idx, yy=yy, fwd=fwd):
                    relay[yy] = send(part.at[idx, pl.ds(0, half)], r0k.at[yy, 0], fwd)

                pend.append(go)
            elif d == (4 - sgn) % 4:

                def go(idx=idx, yy=yy, back=back):
                    direct[yy] = send(part.at[idx, pl.ds(0, half)], r0k.at[yy, 1], back)

                pend.append(go)
            if yy == 1:

                def go(d=d, xx=xx):
                    yfirst[d] = send(
                        part.at[did(xx, 1 - yl, c), pl.ds(half, half)], y1k.at[xx], YN
                    )

                if d in (2, 0):
                    pend.append(go)
            if (d, yy) == (1, 0) or (d, yy) == (3, 1):

                def go(d=d, xx=xx):
                    yfirst[d] = send(
                        part.at[did(xx, 1 - yl, c), pl.ds(half, half)], y1k.at[xx], YN
                    )

                pend.append(go)
            yield
        flush(0)

        def ring_tail(base, n, buf, item, yy, sgn, mine):
            fwd = XP if sgn == 1 else XM
            nxt = xp if sgn == 1 else xm
            ref = part.at[did(nxt, yy, c), pl.ds(base, n)]
            ref[...] = ref[...] + buf[item, 0]
            return send(ref, buf.at[item, 2], fwd)

        merged = {}
        for yy in (0, 1):
            relay[yy].wait_recv()
            merged[yy] = ring_tail(0, half, r0k, yy, yy, 1 if yy == 0 else -1, None)
            yield
        rel1, dir1, mer1 = {}, {}, {}
        for d in (2, 1, 3, 0):
            xx = wrap4(x + d)
            yfirst[d].wait_recv()
            ref = part.at[did(xx, yl, c), pl.ds(half, half)]
            ref[...] = ref[...] + y1k[xx]
            for it, sgn in ((0, 1), (1, -1)):
                fwd, back = (XP, XM) if sgn == 1 else (XM, XP)
                src = part.at[did(xx, yl, c), pl.ds(half + it * quar, quar)]
                if d == 2:
                    rel1[it] = send(src, r1k.at[it, 0], fwd)
                elif d == (4 - sgn) % 4:
                    dir1[it] = send(src, r1k.at[it, 1], back)
            yield
        for yy in (0, 1):
            direct[yy].wait_recv()
            merged[yy].wait_recv()
            obk[yy] = part[did(x, yy, c), pl.ds(0, half)] + r0k[yy, 1] + r0k[yy, 2]
        ysend = send(obk.at[1 - yl], y0k, YN)
        yield
        for it, sgn in ((0, 1), (1, -1)):
            rel1[it].wait_recv()
            mer1[it] = ring_tail(half + it * quar, quar, r1k, it, yl, sgn, None)
            yield
        ysend.wait_recv()
        out(0, half, obk[yl] + y0k[...])
        yield
        for it in (0, 1):
            dir1[it].wait_recv()
            mer1[it].wait_recv()
            base = half + it * quar
            out(base, quar, part[did(x, yl, c), pl.ds(base, quar)] + r1k[it, 1] + r1k[it, 2])
            yield

    def prepare():
        ld_w.wait()
        for g in range(4):

            @pl.loop(0, 4)
            def _(q, g=g):
                at = pl.multiple_of((g * 4 + q) * B, B)
                xw[pl.ds(T, B), pl.ds(at, B)] = xwt[pl.ds(at, B), pl.ds(T, B)].T

            yield
        ld_x.wait()
        for g in range(4):

            @pl.loop(0, 4)
            def _(q, g=g):
                at = pl.multiple_of((g * 4 + q) * B, B)
                xwt[pl.ds(at, B), pl.ds(0, T)] = xw[pl.ds(0, T), pl.ds(at, B)].T

            yield
        ld_c.wait()
        slot = T // len_ref.shape[0]
        for s in range(len_ref.shape[0]):
            keep = lax.broadcasted_iota(jnp.int32, (slot, cot.shape[1]), 0) < len_ref[s]
            cur = cot[pl.ds(s * slot, slot)].astype(F32)
            cot[pl.ds(s * slot, slot)] = jnp.where(keep, cur, 0.0).astype(BF)
            yield

    drive(gather_dp(rhi), prepare())

    KG = 1024

    def rotate(r):
        @pl.loop(0, xw.shape[1] // KG)
        def _(g):
            at = pl.multiple_of(g * KG, KG)
            s32[...] += nn(xw[:, pl.ds(at, KG)], r[pl.ds(at, KG)])

    s32[...] = jnp.zeros_like(s32)
    rotate(rhi)
    sq = s32[...]
    sq = sq * sq
    NS = s32.shape[0] // 128
    sums = jnp.sum((sq[:, :128] + sq[:, 128:]).T, axis=0, keepdims=True)
    for g in range(NS):
        stat_mine[pl.ds(g, 1)] = sums[:, g * 128 : (g + 1) * 128]
    for g in range(NS, 8):
        stat_mine[pl.ds(g, 1)] = jnp.zeros((1, 128), F32)
    stats = []
    for d in range(1, 16):
        stats.append(
            send(stat_mine, stat_all.at[d], {"dp": i, "loop": lax.rem(j + d, 16)})
        )
    for cp in stats:
        cp.wait_recv()
    power = stat_mine[...]
    for d in range(1, 16):
        power = power + stat_all[d]
    limit = CLIP_RATIO * jnp.sqrt(power * inv_width + EPS_POWER)
    for g in range(NS):
        lim = jnp.broadcast_to(limit[g : g + 1, :], (128, 128)).T
        for h in (0, 1):
            v = s32[pl.ds(g * 128, 128), pl.ds(h * 128, 128)]
            v = jnp.minimum(jnp.maximum(v, -lim), lim)
            if g * 128 < T:
                aqt[pl.ds(h * 128, 128), pl.ds(g * 128, 128)] = v.T.astype(BF)
            else:
                at = pl.multiple_of(i * B + (g * 128 - T), 128)
                mqt[pl.ds(at, 128), pl.ds(h * 128, 128)] = v.astype(BF)

    drive(gather_dp(mqt))

    ga = nn(cot[:, pl.ds(0, KG)], mqt[pl.ds(0, KG)])
    for g in range(1, 4):
        ga = ga + nn(cot[:, pl.ds(g * KG, KG)], mqt[pl.ds(g * KG, KG)])
    gam[pl.ds(0, T)] = ga.astype(BF)
    gat_all[j] = ga.T.astype(BF)

    def chunk_gm(idx):
        return nn(aqt[...], cot[:, pl.ds(pl.multiple_of(idx * B, B), B)])

    def out_gm(at, n, v):
        gm_all[j, pl.ds(at, n)] = v.astype(BF)
        gout[pl.ds(at, n)] = v

    drive(reduce_dp(0, part_a, chunk_gm, out_gm), gather_loop(gat_all), gather_loop(r_all))
    gam[pl.ds(T, B)] = gout[...].T.astype(BF)

    def chunk_g(idx):
        return nn(xwt[pl.ds(pl.multiple_of(idx * B, B), B)], gam[...])

    def out_g(at, n, v):
        gout[pl.ds(at, n)] = v * scale

    drive(gather_loop(gm_all), reduce_dp(1, part_b, chunk_g, out_g), gather_dp(rlo))
    rotate(rlo)
    sh, sl = split(s32[...])
    s_hi[...] = sh
    s_lo[...] = sl
    for cp in sent:
        cp.wait_send()
    sent.clear()

    def chunk_c(idx):
        a, b = gat_all[idx], gm_all[idx]
        return (
            nn(a, s_hi[pl.ds(0, T)])
            + nn(a, s_lo[pl.ds(0, T)])
            + nn(b, s_hi[pl.ds(T, B)])
            + nn(b, s_lo[pl.ds(T, B)])
        )

    def out_c(at, n, v):
        cross[pl.ds(pl.multiple_of(i * B + at, B // 4), n)] = v * scale

    drive(reduce_dp(2, part_a, chunk_c, out_c))
    drive(gather_dp(cross))

    @pl.loop(0, KB)
    def _(k):
        ah, al = split(r_all[k])
        bh, bl = split(cross[pl.ds(pl.multiple_of(k * B, B), B)])
        gout[...] -= nn(ah, bh) + nn(ah, bl) + nn(al, bh)

    out_ref[...] = gout[...]
    for cp in sent:
        cp.wait_send()


def solution(mesh):
    def on_device(tokens, cotangent, proj_weight, rotation, doc_lengths):
        T, D = tokens.shape
        B = rotation.shape[1]
        n = mesh.shape["dp"]
        hbm = pl.BlockSpec(memory_space=pl.ANY)
        total = T * n
        V = pltpu.VMEM

        def body(*refs):
            kernel(1.0 / D, 1.0 / (float(total) ** 0.5), *refs)

        return pl.pallas_call(
            body,
            out_shape=jax.ShapeDtypeStruct((B, B), F32),
            in_specs=[pl.BlockSpec(memory_space=pltpu.SMEM), hbm, hbm, hbm, hbm],
            out_specs=pl.BlockSpec(memory_space=pltpu.VMEM),
            scratch_shapes=[
                V((T + B, D), BF),
                V((D, T + B), BF),
                V((T, D), BF),
                V((D, B), BF),
                V((D, B), BF),
                V((D, B), BF),
                V((T + B, B), F32),
                V((T + B, B), BF),
                V((T + B, B), BF),
                V((8, 128), F32),
                V((16, 8, 128), F32),
                V((T + B, B), BF),
                V((B, T), BF),
                V((16, B, T), BF),
                V((16, B, B), BF),
                V((16, B, B), F32),
                V((16, B, B), F32),
                V((16, B, B), F32),
                V((3, 8, B, B), F32),
                V((3, 2, 3, B // 2, B), F32),
                V((3, 2, 3, B // 4, B), F32),
                V((3, B // 2, B), F32),
                V((3, 4, B // 2, B), F32),
                V((3, 2, B // 2, B), F32),
                V((B, B), F32),
                V((D, B), F32),
                pltpu.SemaphoreType.DMA((SEMS,)),
                pltpu.SemaphoreType.DMA((SEMS,)),
                pltpu.SemaphoreType.DMA((4,)),
            ],
            compiler_params=pltpu.CompilerParams(
                collective_id=0, has_side_effects=True, vmem_limit_bytes=67000000
            ),
        )(doc_lengths, tokens, cotangent, proj_weight, rotation)

    in_specs = (P("dp", None), P("dp", None), P(None, "dp"), P("dp", "loop"), P("dp"))
    return jax.shard_map(
        on_device, mesh=mesh, in_specs=in_specs, out_specs=P("dp", "loop"), check_vma=False
    )
```

```python
import jax
import jax.numpy as jnp
from jax import lax
from jax.experimental import pallas as pl
from jax.experimental.pallas import tpu as pltpu
from jax.sharding import PartitionSpec as P

MESH = pl.DeviceIdType.MESH
BF = jnp.bfloat16
F32 = jnp.float32
CLIP_RATIO = 2.0
EPS_POWER = 1e-06
SEMS = 256


def nn(a, b):
    return lax.dot_general(a, b, (((1,), (0,)), ((), ())), preferred_element_type=F32)


def split(v):
    hi = v.astype(BF)
    return hi, (v - hi.astype(F32)).astype(BF)


def advance(gen, steps):
    for _ in range(steps):
        if next(gen, StopIteration) is StopIteration:
            return False
    return True


def drive(*main, beside=None):
    live = list(main)
    while live:
        for item in list(live):
            if not advance(*item):
                live.remove(item)
        if beside is not None:
            advance(*beside)


def chain(*gens):
    for g in gens:
        yield from g


def kernel(
    inv_width,
    scale,
    len_ref,
    tok_hbm,
    cot_hbm,
    w_hbm,
    rot_hbm,
    out_ref,
    xw,
    xwt,
    cot,
    rhi,
    rlo,
    mqt,
    s32,
    s_hi,
    s_lo,
    stat_mine,
    stat_all,
    gam,
    aqt,
    gat_all,
    gm_all,
    r_all,
    part_a,
    part_b,
    rc,
    rx0,
    rx1,
    ry0,
    ry1,
    ob,
    gout,
    cross,
    ssem,
    rsem,
    lsem,
    tok,
):
    i = lax.axis_index("dp")
    j = lax.axis_index("loop")
    x, yl, c = i // 4, (i // 2) % 2, i % 2
    yh, z = j // 8, j % 8
    T = tok_hbm.shape[0]
    B = 256
    KB = 16

    def wrap4(v):
        return lax.rem(v + 4, 4)

    def wrap8(v):
        return lax.rem(v + 8, 8)

    xp, xm = wrap4(x + 1), wrap4(x - 1)
    x2 = wrap4(x + 2)
    XP = {"dp": xp * 4 + yl * 2 + c, "loop": j}
    XM = {"dp": xm * 4 + yl * 2 + c, "loop": j}
    YN = {"dp": x * 4 + (1 - yl) * 2 + c, "loop": j}
    CORE = {"dp": x * 4 + yl * 2 + (1 - c), "loop": j}
    zp, zm = wrap8(z + 1), wrap8(z - 1)
    ZP = {"dp": i, "loop": yh * 8 + zp}
    ZM = {"dp": i, "loop": yh * 8 + zm}
    YH = {"dp": i, "loop": (1 - yh) * 8 + z}

    def did(xx, yy, cc):
        return xx * 4 + yy * 2 + cc

    counter = [0]
    sent = []

    def send(src, dst, dev):
        k = counter[0]
        counter[0] += 1
        cp = pltpu.make_async_remote_copy(
            src_ref=src,
            dst_ref=dst,
            send_sem=ssem.at[k],
            recv_sem=rsem.at[k],
            device_id=dev,
            device_id_type=MESH,
        )
        cp.start()
        sent.append(cp)
        return cp

    def send_same(ref, dev):
        return send(ref, ref, dev)

    ld_r = pltpu.make_async_copy(rot_hbm, r_all.at[j], lsem.at[0])
    ld_x = pltpu.make_async_copy(tok_hbm, xw.at[pl.ds(0, T)], lsem.at[1])
    ld_w = pltpu.make_async_copy(w_hbm, xwt.at[:, pl.ds(T, B)], lsem.at[2])
    ld_c = pltpu.make_async_copy(cot_hbm, cot, lsem.at[3])
    ld_r.start()
    ld_w.start()
    ld_x.start()
    ld_c.start()

    barrier = pltpu.get_barrier_semaphore()
    for dev in (XP, XM, YN, CORE, ZP, ZM, YH):
        pl.semaphore_signal(barrier, inc=1, device_id=dev, device_id_type=MESH)
    ld_r.wait()
    rv = r_all[j]
    hv, lv = split(rv)
    own_rows = pl.ds(pl.multiple_of(i * B, B), B)
    rhi[own_rows] = hv
    rlo[own_rows] = lv
    pl.semaphore_wait(barrier, 7)

    def rows(buf, idx, part=None):
        if part is None:
            return buf.at[pl.ds(pl.multiple_of(idx * B, B), B)]
        return buf.at[pl.ds(pl.multiple_of(idx * B + part * (B // 2), B // 2), B // 2)]

    def gather_dp(buf):
        own = rows(buf, i)
        a_y = send_same(own, YN)
        a_p = send_same(own, XP)
        a_m = send_same(own, XM)
        core = [send_same(own, CORE)]
        left, right, opp = did(xm, yl, c), did(xp, yl, c), did(x2, yl, c)
        ynb = did(x, 1 - yl, c)
        yield
        a_p.wait_recv()
        r_p = send_same(rows(buf, left, 0), XP)
        y_l = send_same(rows(buf, left, 1), YN)
        core.append(send_same(rows(buf, left), CORE))
        yield
        a_m.wait_recv()
        r_m = send_same(rows(buf, right, 1), XM)
        y_r = send_same(rows(buf, right, 0), YN)
        core.append(send_same(rows(buf, right), CORE))
        yield
        a_y.wait_recv()
        d_p = send_same(rows(buf, ynb, 0), XP)
        d_m = send_same(rows(buf, ynb, 1), XM)
        core.append(send_same(rows(buf, ynb), CORE))
        yield
        r_p.wait_recv()
        y_a = send_same(rows(buf, opp, 0), YN)
        core.append(send_same(rows(buf, opp, 0), CORE))
        yield
        r_m.wait_recv()
        y_b = send_same(rows(buf, opp, 1), YN)
        core.append(send_same(rows(buf, opp, 1), CORE))
        yield
        lft2, rgt2, opp2 = did(xm, 1 - yl, c), did(xp, 1 - yl, c), did(x2, 1 - yl, c)
        for cp, ref in (
            (d_p, rows(buf, lft2, 0)),
            (d_m, rows(buf, rgt2, 1)),
            (y_l, rows(buf, lft2, 1)),
            (y_r, rows(buf, rgt2, 0)),
            (y_a, rows(buf, opp2, 0)),
            (y_b, rows(buf, opp2, 1)),
        ):
            cp.wait_recv()
            core.append(send_same(ref, CORE))
            yield
        for cp in core:
            cp.wait_recv()

    def gather_loop(buf):
        half = B // 2

        def blk(u, zz, part=None):
            ref = buf.at[u * 8 + zz]
            if part is None:
                return ref
            return ref.at[pl.ds(part * half, half)]

        own = blk(yh, z)
        oth = send_same(own, YH)
        wp = {0: send_same(own, ZP)}
        wm = {0: send_same(own, ZM)}
        lanes = (yh, 1 - yh)
        yield
        oth.wait_recv()
        wp[1] = send_same(blk(lanes[1], z), ZP)
        wm[1] = send_same(blk(lanes[1], z), ZM)
        yield
        for d in range(1, 5):
            for ln in (0, 1):
                wp[ln].wait_recv()
                if d < 4:
                    ref = blk(lanes[ln], wrap8(z - d), None if d < 3 else 0)
                    wp[ln] = send_same(ref, ZP)
                yield
                wm[ln].wait_recv()
                if d < 4:
                    ref = blk(lanes[ln], wrap8(z + d), None if d < 3 else 1)
                    wm[ln] = send_same(ref, ZM)
                yield

    def reduce_dp(k, part, chunk, out):
        rck, r0k, r1k, y0k, y1k, obk = (b.at[k] for b in (rc, rx0, rx1, ry0, ry1, ob))
        order = [(2, 0), (2, 1), (3, 0), (1, 1), (1, 0), (3, 1), (0, 0), (0, 1)]
        half, quar = B // 2, B // 4
        pend = []

        def flush(keep):
            while len(pend) > keep:
                pend.pop(0)()

        core = {}
        for d, yy in order:
            xx = wrap4(x + d)
            idx = did(xx, yy, 1 - c)
            part[idx] = chunk(idx)

            def go(idx=idx, d=d, yy=yy, xx=xx):
                core[d, yy] = send(part.at[idx], rck.at[xx * 2 + yy], CORE)

            pend.append(go)
            flush(1)
            yield
        relay, direct, yfirst = {}, {}, {}
        for d, yy in order:
            xx = wrap4(x + d)
            idx = did(xx, yy, c)
            v = chunk(idx)
            flush(0)
            core[d, yy].wait_recv()
            part[idx] = v + rck[xx * 2 + yy]
            sgn = 1 if yy == 0 else -1
            fwd, back = (XP, XM) if sgn == 1 else (XM, XP)
            if d == 2:

                def go(idx=idx, yy=yy, fwd=fwd):
                    relay[yy] = send(part.at[idx, pl.ds(0, half)], r0k.at[yy, 0], fwd)

                pend.append(go)
            elif d == (4 - sgn) % 4:

                def go(idx=idx, yy=yy, back=back):
                    direct[yy] = send(part.at[idx, pl.ds(0, half)], r0k.at[yy, 1], back)

                pend.append(go)
            if yy == 1:

                def go(d=d, xx=xx):
                    yfirst[d] = send(
                        part.at[did(xx, 1 - yl, c), pl.ds(half, half)], y1k.at[xx], YN
                    )

                if d in (2, 0):
                    pend.append(go)
            if (d, yy) == (1, 0) or (d, yy) == (3, 1):

                def go(d=d, xx=xx):
                    yfirst[d] = send(
                        part.at[did(xx, 1 - yl, c), pl.ds(half, half)], y1k.at[xx], YN
                    )

                pend.append(go)
            yield
        flush(0)

        def ring_tail(base, n, buf, item, yy, sgn, mine):
            fwd = XP if sgn == 1 else XM
            nxt = xp if sgn == 1 else xm
            ref = part.at[did(nxt, yy, c), pl.ds(base, n)]
            ref[...] = ref[...] + buf[item, 0]
            return send(ref, buf.at[item, 2], fwd)

        merged = {}
        for yy in (0, 1):
            relay[yy].wait_recv()
            merged[yy] = ring_tail(0, half, r0k, yy, yy, 1 if yy == 0 else -1, None)
            yield
        rel1, dir1, mer1 = {}, {}, {}
        for d in (2, 1, 3, 0):
            xx = wrap4(x + d)
            yfirst[d].wait_recv()
            ref = part.at[did(xx, yl, c), pl.ds(half, half)]
            ref[...] = ref[...] + y1k[xx]
            for it, sgn in ((0, 1), (1, -1)):
                fwd, back = (XP, XM) if sgn == 1 else (XM, XP)
                src = part.at[did(xx, yl, c), pl.ds(half + it * quar, quar)]
                if d == 2:
                    rel1[it] = send(src, r1k.at[it, 0], fwd)
                elif d == (4 - sgn) % 4:
                    dir1[it] = send(src, r1k.at[it, 1], back)
            yield
        for yy in (0, 1):
            direct[yy].wait_recv()
            merged[yy].wait_recv()
            obk[yy] = part[did(x, yy, c), pl.ds(0, half)] + r0k[yy, 1] + r0k[yy, 2]
        ysend = send(obk.at[1 - yl], y0k, YN)
        yield
        for it, sgn in ((0, 1), (1, -1)):
            rel1[it].wait_recv()
            mer1[it] = ring_tail(half + it * quar, quar, r1k, it, yl, sgn, None)
            yield
        ysend.wait_recv()
        out(0, half, obk[yl] + y0k[...])
        yield
        for it in (0, 1):
            dir1[it].wait_recv()
            mer1[it].wait_recv()
            base = half + it * quar
            out(base, quar, part[did(x, yl, c), pl.ds(base, quar)] + r1k[it, 1] + r1k[it, 2])
            yield

    def entered():
        for r in range(3):
            for dev in (ZP, ZM):
                pl.semaphore_signal(tok.at[r], inc=1, device_id=dev, device_id_type=MESH)
            yield
            pl.semaphore_wait(tok.at[r], 2)
        pl.semaphore_signal(tok.at[3], inc=1, device_id=YH, device_id_type=MESH)
        yield
        pl.semaphore_wait(tok.at[3], 1)

    def prepare():
        ld_w.wait()
        for g in range(4):

            @pl.loop(0, 4)
            def _(q, g=g):
                at = pl.multiple_of((g * 4 + q) * B, B)
                xw[pl.ds(T, B), pl.ds(at, B)] = xwt[pl.ds(at, B), pl.ds(T, B)].T

            yield
        ld_x.wait()
        for g in range(4):

            @pl.loop(0, 4)
            def _(q, g=g):
                at = pl.multiple_of((g * 4 + q) * B, B)
                xwt[pl.ds(at, B), pl.ds(0, T)] = xw[pl.ds(0, T), pl.ds(at, B)].T

            yield
        ld_c.wait()
        slot = T // len_ref.shape[0]
        for s in range(len_ref.shape[0]):
            keep = lax.broadcasted_iota(jnp.int32, (slot, cot.shape[1]), 0) < len_ref[s]
            cur = cot[pl.ds(s * slot, slot)].astype(F32)
            cot[pl.ds(s * slot, slot)] = jnp.where(keep, cur, 0.0).astype(BF)
            yield

    ring_r = gather_loop(r_all)
    first = gather_dp(rhi)
    advance(first, 1)
    advance(ring_r, 1)
    drive((first, 1), (prepare(), 1), (entered(), 1))
    advance(ring_r, 1)

    KG = 1024

    def rotate(r):
        @pl.loop(0, xw.shape[1] // KG)
        def _(g):
            at = pl.multiple_of(g * KG, KG)
            s32[...] += nn(xw[:, pl.ds(at, KG)], r[pl.ds(at, KG)])

        yield

    s32[...] = jnp.zeros_like(s32)
    drive((rotate(rhi), 1))
    sq = s32[...]
    sq = sq * sq
    NS = s32.shape[0] // 128
    sums = jnp.sum((sq[:, :128] + sq[:, 128:]).T, axis=0, keepdims=True)
    for g in range(NS):
        stat_mine[pl.ds(g, 1)] = sums[:, g * 128 : (g + 1) * 128]
    for g in range(NS, 8):
        stat_mine[pl.ds(g, 1)] = jnp.zeros((1, 128), F32)
    stats = []
    for d in range(1, 16):
        stats.append(
            send(stat_mine, stat_all.at[d], {"dp": i, "loop": lax.rem(j + d, 16)})
        )
    for cp in stats:
        cp.wait_recv()
    power = stat_mine[...]
    for d in range(1, 16):
        power = power + stat_all[d]
    limit = CLIP_RATIO * jnp.sqrt(power * inv_width + EPS_POWER)
    for g in range(NS):
        lim = jnp.broadcast_to(limit[g : g + 1, :], (128, 128)).T
        for h in (0, 1):
            v = s32[pl.ds(g * 128, 128), pl.ds(h * 128, 128)]
            v = jnp.minimum(jnp.maximum(v, -lim), lim)
            if g * 128 < T:
                aqt[pl.ds(h * 128, 128), pl.ds(g * 128, 128)] = v.T.astype(BF)
            else:
                at = pl.multiple_of(i * B + (g * 128 - T), 128)
                mqt[pl.ds(at, 128), pl.ds(h * 128, 128)] = v.astype(BF)

    advance(ring_r, 4)
    drive((gather_dp(mqt), 1))

    ga = nn(cot[:, pl.ds(0, KG)], mqt[pl.ds(0, KG)])
    for g in range(1, 4):
        ga = ga + nn(cot[:, pl.ds(g * KG, KG)], mqt[pl.ds(g * KG, KG)])
    gam[pl.ds(0, T)] = ga.astype(BF)
    gat_all[j] = ga.T.astype(BF)

    def chunk_gm(idx):
        return nn(aqt[...], cot[:, pl.ds(pl.multiple_of(idx * B, B), B)])

    def out_gm(at, n, v):
        gm_all[j, pl.ds(at, n)] = v.astype(BF)
        gout[pl.ds(at, n)] = v

    ring_ga, ring_gm = gather_loop(gat_all), gather_loop(gm_all)
    advance(ring_ga, 1)
    drive((reduce_dp(0, part_a, chunk_gm, out_gm), 3), beside=(ring_ga, 1))
    advance(ring_gm, 1)
    gam[pl.ds(T, B)] = gout[...].T.astype(BF)

    def chunk_g(idx):
        return nn(xwt[pl.ds(pl.multiple_of(idx * B, B), B)], gam[...])

    def out_g(at, n, v):
        gout[pl.ds(at, n)] = v * scale

    rings = chain(ring_ga, ring_gm)
    drive((reduce_dp(1, part_b, chunk_g, out_g), 3), beside=(rings, 1))
    drive((chain(gather_dp(rlo), rotate(rlo)), 1), (rings, 1))
    sh, sl = split(s32[...])
    s_hi[...] = sh
    s_lo[...] = sl
    for cp in sent:
        cp.wait_send()
    sent.clear()

    def chunk_c(idx):
        a, b = gat_all[idx], gm_all[idx]
        return (
            nn(a, s_hi[pl.ds(0, T)])
            + nn(a, s_lo[pl.ds(0, T)])
            + nn(b, s_hi[pl.ds(T, B)])
            + nn(b, s_lo[pl.ds(T, B)])
        )

    def out_c(at, n, v):
        cross[pl.ds(pl.multiple_of(i * B + at, B // 4), n)] = v * scale

    drive((reduce_dp(2, part_a, chunk_c, out_c), 3), beside=(ring_r, 1))
    drive((gather_dp(cross), 2), (ring_r, 1))

    @pl.loop(0, KB)
    def _(k):
        ah, al = split(r_all[k])
        bh, bl = split(cross[pl.ds(pl.multiple_of(k * B, B), B)])
        gout[...] -= nn(ah, bh) + nn(ah, bl) + nn(al, bh)

    out_ref[...] = gout[...]
    for cp in sent:
        cp.wait_send()


def solution(mesh):
    def on_device(tokens, cotangent, proj_weight, rotation, doc_lengths):
        T, D = tokens.shape
        B = rotation.shape[1]
        n = mesh.shape["dp"]
        hbm = pl.BlockSpec(memory_space=pl.ANY)
        total = T * n
        V = pltpu.VMEM

        def body(*refs):
            kernel(1.0 / D, 1.0 / (float(total) ** 0.5), *refs)

        return pl.pallas_call(
            body,
            out_shape=jax.ShapeDtypeStruct((B, B), F32),
            in_specs=[pl.BlockSpec(memory_space=pltpu.SMEM), hbm, hbm, hbm, hbm],
            out_specs=pl.BlockSpec(memory_space=pltpu.VMEM),
            scratch_shapes=[
                V((T + B, D), BF),
                V((D, T + B), BF),
                V((T, D), BF),
                V((D, B), BF),
                V((D, B), BF),
                V((D, B), BF),
                V((T + B, B), F32),
                V((T + B, B), BF),
                V((T + B, B), BF),
                V((8, 128), F32),
                V((16, 8, 128), F32),
                V((T + B, B), BF),
                V((B, T), BF),
                V((16, B, T), BF),
                V((16, B, B), BF),
                V((16, B, B), F32),
                V((16, B, B), F32),
                V((16, B, B), F32),
                V((3, 8, B, B), F32),
                V((3, 2, 3, B // 2, B), F32),
                V((3, 2, 3, B // 4, B), F32),
                V((3, B // 2, B), F32),
                V((3, 4, B // 2, B), F32),
                V((3, 2, B // 2, B), F32),
                V((B, B), F32),
                V((D, B), F32),
                pltpu.SemaphoreType.DMA((SEMS,)),
                pltpu.SemaphoreType.DMA((SEMS,)),
                pltpu.SemaphoreType.DMA((4,)),
                pltpu.SemaphoreType.REGULAR((4,)),
            ],
            compiler_params=pltpu.CompilerParams(
                collective_id=0, has_side_effects=True, vmem_limit_bytes=67000000
            ),
        )(doc_lengths, tokens, cotangent, proj_weight, rotation)

    in_specs = (P("dp", None), P("dp", None), P(None, "dp"), P("dp", "loop"), P("dp"))
    return jax.shard_map(
        on_device, mesh=mesh, in_specs=in_specs, out_specs=P("dp", "loop"), check_vma=False
    )
```

```python
import jax
import jax.numpy as jnp
from jax import lax
from jax.experimental import pallas as pl
from jax.experimental.pallas import tpu as pltpu
from jax.sharding import PartitionSpec as P

MESH = pl.DeviceIdType.MESH
BF = jnp.bfloat16
F32 = jnp.float32
CLIP_RATIO = 2.0
EPS_POWER = 1e-06
SEMS = 256


def nn(a, b):
    return lax.dot_general(a, b, (((1,), (0,)), ((), ())), preferred_element_type=F32)


def split(v):
    hi = v.astype(BF)
    return hi, (v - hi.astype(F32)).astype(BF)


def advance(gen, steps):
    for _ in range(steps):
        if next(gen, StopIteration) is StopIteration:
            return False
    return True


def drive(*main, beside=None):
    live = list(main)
    while live:
        for item in list(live):
            if not advance(*item):
                live.remove(item)
        if beside is not None:
            advance(*beside)


def chain(*gens):
    for g in gens:
        yield from g


def kernel(
    inv_width,
    scale,
    len_ref,
    tok_hbm,
    cot_hbm,
    w_hbm,
    rot_hbm,
    out_ref,
    xw,
    xwt,
    cot,
    rhi,
    rlo,
    mqt,
    s32,
    s_hi,
    s_lo,
    stat_mine,
    stat_all,
    gam,
    aqt,
    gat_all,
    gm_all,
    r_all,
    part_a,
    part_b,
    rc,
    rx0,
    rx1,
    ry0,
    ry1,
    ob,
    gout,
    cross,
    ssem,
    rsem,
    lsem,
    tok,
    ga32,
):
    i = lax.axis_index("dp")
    j = lax.axis_index("loop")
    x, yl, c = i // 4, (i // 2) % 2, i % 2
    yh, z = j // 8, j % 8
    T = tok_hbm.shape[0]
    B = 256

    def wrap4(v):
        return lax.rem(v + 4, 4)

    def wrap8(v):
        return lax.rem(v + 8, 8)

    xp, xm = wrap4(x + 1), wrap4(x - 1)
    x2 = wrap4(x + 2)
    XP = {"dp": xp * 4 + yl * 2 + c, "loop": j}
    XM = {"dp": xm * 4 + yl * 2 + c, "loop": j}
    YN = {"dp": x * 4 + (1 - yl) * 2 + c, "loop": j}
    CORE = {"dp": x * 4 + yl * 2 + (1 - c), "loop": j}
    zp, zm = wrap8(z + 1), wrap8(z - 1)
    ZP = {"dp": i, "loop": yh * 8 + zp}
    ZM = {"dp": i, "loop": yh * 8 + zm}
    YH = {"dp": i, "loop": (1 - yh) * 8 + z}

    def did(xx, yy, cc):
        return xx * 4 + yy * 2 + cc

    counter = [0]
    sent = []

    def send(src, dst, dev):
        k = counter[0]
        counter[0] += 1
        cp = pltpu.make_async_remote_copy(
            src_ref=src,
            dst_ref=dst,
            send_sem=ssem.at[k],
            recv_sem=rsem.at[k],
            device_id=dev,
            device_id_type=MESH,
        )
        cp.start()
        sent.append(cp)
        return cp

    def send_same(ref, dev):
        return send(ref, ref, dev)

    ld_r = pltpu.make_async_copy(rot_hbm, r_all.at[j], lsem.at[0])
    ld_x = pltpu.make_async_copy(tok_hbm, xw.at[pl.ds(0, T)], lsem.at[1])
    ld_w = pltpu.make_async_copy(w_hbm, xwt.at[:, pl.ds(T, B)], lsem.at[2])
    ld_c = pltpu.make_async_copy(cot_hbm, cot, lsem.at[3])
    ld_r.start()
    ld_w.start()
    ld_x.start()
    ld_c.start()

    barrier = pltpu.get_barrier_semaphore()
    for dev in (XP, XM, YN, CORE, ZP, ZM, YH):
        pl.semaphore_signal(barrier, inc=1, device_id=dev, device_id_type=MESH)
    ld_r.wait()
    rv = r_all[j]
    hv, lv = split(rv)
    own_rows = pl.ds(pl.multiple_of(i * B, B), B)
    rhi[own_rows] = hv
    rlo[own_rows] = lv
    pl.semaphore_wait(barrier, 7)

    def rows(buf, idx, part=None):
        if part is None:
            return buf.at[pl.ds(pl.multiple_of(idx * B, B), B)]
        return buf.at[pl.ds(pl.multiple_of(idx * B + part * (B // 2), B // 2), B // 2)]

    def gather_dp(buf, use):
        left, right, opp = did(xm, yl, c), did(xp, yl, c), did(x2, yl, c)
        ynb = did(x, 1 - yl, c)
        lft2, rgt2, opp2 = did(xm, 1 - yl, c), did(xp, 1 - yl, c), did(x2, 1 - yl, c)
        core = []

        def pair(ref, xx=None, yy=None):
            core.append((send_same(ref, CORE), None if xx is None else did(xx, yy, 1 - c)))

        def meet(n):
            for _ in range(n):
                cp, idx = core.pop(0)
                cp.wait_recv()
                if idx is not None:
                    use(idx)

        a_y0 = send_same(rows(buf, i, 0), YN)
        a_p0 = send_same(rows(buf, i, 0), XP)
        a_m1 = send_same(rows(buf, i, 1), XM)
        a_y1 = send_same(rows(buf, i, 1), YN)
        a_p1 = send_same(rows(buf, i, 1), XP)
        a_m0 = send_same(rows(buf, i, 0), XM)
        pair(rows(buf, i), x, yl)
        yield
        use(i)
        a_p0.wait_recv()
        r_p = send_same(rows(buf, left, 0), XP)
        a_m1.wait_recv()
        r_m = send_same(rows(buf, right, 1), XM)
        yield
        a_y0.wait_recv()
        d_p = send_same(rows(buf, ynb, 0), XP)
        a_y1.wait_recv()
        d_m = send_same(rows(buf, ynb, 1), XM)
        yield
        a_p1.wait_recv()
        y_l = send_same(rows(buf, left, 1), YN)
        pair(rows(buf, left), xm, yl)
        a_m0.wait_recv()
        y_r = send_same(rows(buf, right, 0), YN)
        pair(rows(buf, right), xp, yl)
        pair(rows(buf, ynb), x, 1 - yl)
        use(left)
        yield
        r_p.wait_recv()
        y_a = send_same(rows(buf, opp, 0), YN)
        r_m.wait_recv()
        y_b = send_same(rows(buf, opp, 1), YN)
        pair(rows(buf, opp), x2, yl)
        use(right)
        use(ynb)
        meet(1)
        yield
        use(opp)
        meet(1)
        yield
        d_p.wait_recv()
        y_l.wait_recv()
        pair(rows(buf, lft2), xm, 1 - yl)
        use(lft2)
        yield
        d_m.wait_recv()
        y_r.wait_recv()
        pair(rows(buf, rgt2), xp, 1 - yl)
        use(rgt2)
        meet(2)
        yield
        y_a.wait_recv()
        pair(rows(buf, opp2, 0))
        meet(1)
        yield
        y_b.wait_recv()
        pair(rows(buf, opp2, 1), x2, 1 - yl)
        use(opp2)
        meet(len(core))

    def gather_loop(buf):
        half = B // 2

        def blk(u, zz, part=None):
            ref = buf.at[u * 8 + zz]
            if part is None:
                return ref
            return ref.at[pl.ds(part * half, half)]

        own = blk(yh, z)
        oth = send_same(own, YH)
        wp = {0: send_same(own, ZP)}
        wm = {0: send_same(own, ZM)}
        lanes = (yh, 1 - yh)
        yield
        oth.wait_recv()
        wp[1] = send_same(blk(lanes[1], z), ZP)
        wm[1] = send_same(blk(lanes[1], z), ZM)
        yield
        for d in range(1, 5):
            for ln in (0, 1):
                wp[ln].wait_recv()
                if d < 4:
                    ref = blk(lanes[ln], wrap8(z - d), None if d < 3 else 0)
                    wp[ln] = send_same(ref, ZP)
                yield
                wm[ln].wait_recv()
                if d < 4:
                    ref = blk(lanes[ln], wrap8(z + d), None if d < 3 else 1)
                    wm[ln] = send_same(ref, ZM)
                yield

    def reduce_dp(k, part, chunk, out):
        rck, r0k, r1k, y0k, y1k, obk = (b.at[k] for b in (rc, rx0, rx1, ry0, ry1, ob))
        order = [(2, 0), (2, 1), (3, 0), (1, 1), (1, 0), (3, 1), (0, 0), (0, 1)]
        half, quar = B // 2, B // 4
        pend = []

        def flush(keep):
            while len(pend) > keep:
                pend.pop(0)()

        core = {}
        for d, yy in order:
            xx = wrap4(x + d)
            idx = did(xx, yy, 1 - c)
            part[idx] = chunk(idx)

            def go(idx=idx, d=d, yy=yy, xx=xx):
                core[d, yy] = send(part.at[idx], rck.at[xx * 2 + yy], CORE)

            pend.append(go)
            flush(1)
            yield
        relay, direct, yfirst = {}, {}, {}
        for d, yy in order:
            xx = wrap4(x + d)
            idx = did(xx, yy, c)
            v = chunk(idx)
            flush(0)
            core[d, yy].wait_recv()
            part[idx] = v + rck[xx * 2 + yy]
            sgn = 1 if yy == 0 else -1
            fwd, back = (XP, XM) if sgn == 1 else (XM, XP)
            if d == 2:

                def go(idx=idx, yy=yy, fwd=fwd):
                    relay[yy] = send(part.at[idx, pl.ds(0, half)], r0k.at[yy, 0], fwd)

                pend.append(go)
            elif d == (4 - sgn) % 4:

                def go(idx=idx, yy=yy, back=back):
                    direct[yy] = send(part.at[idx, pl.ds(0, half)], r0k.at[yy, 1], back)

                pend.append(go)
            if yy == 1:

                def go(d=d, xx=xx):
                    yfirst[d] = send(
                        part.at[did(xx, 1 - yl, c), pl.ds(half, half)], y1k.at[xx], YN
                    )

                if d in (2, 0):
                    pend.append(go)
            if (d, yy) == (1, 0) or (d, yy) == (3, 1):

                def go(d=d, xx=xx):
                    yfirst[d] = send(
                        part.at[did(xx, 1 - yl, c), pl.ds(half, half)], y1k.at[xx], YN
                    )

                pend.append(go)
            yield
        flush(0)

        def ring_tail(base, n, buf, item, yy, sgn, mine):
            fwd = XP if sgn == 1 else XM
            nxt = xp if sgn == 1 else xm
            ref = part.at[did(nxt, yy, c), pl.ds(base, n)]
            ref[...] = ref[...] + buf[item, 0]
            return send(ref, buf.at[item, 2], fwd)

        merged = {}
        for yy in (0, 1):
            relay[yy].wait_recv()
            merged[yy] = ring_tail(0, half, r0k, yy, yy, 1 if yy == 0 else -1, None)
            yield
        rel1, dir1, mer1 = {}, {}, {}
        for d in (2, 1, 3, 0):
            xx = wrap4(x + d)
            yfirst[d].wait_recv()
            ref = part.at[did(xx, yl, c), pl.ds(half, half)]
            ref[...] = ref[...] + y1k[xx]
            for it, sgn in ((0, 1), (1, -1)):
                fwd, back = (XP, XM) if sgn == 1 else (XM, XP)
                src = part.at[did(xx, yl, c), pl.ds(half + it * quar, quar)]
                if d == 2:
                    rel1[it] = send(src, r1k.at[it, 0], fwd)
                elif d == (4 - sgn) % 4:
                    dir1[it] = send(src, r1k.at[it, 1], back)
            yield
        for yy in (0, 1):
            direct[yy].wait_recv()
            merged[yy].wait_recv()
            obk[yy] = part[did(x, yy, c), pl.ds(0, half)] + r0k[yy, 1] + r0k[yy, 2]
        ysend = send(obk.at[1 - yl], y0k, YN)
        yield
        for it, sgn in ((0, 1), (1, -1)):
            rel1[it].wait_recv()
            mer1[it] = ring_tail(half + it * quar, quar, r1k, it, yl, sgn, None)
            yield
        ysend.wait_recv()
        out(0, half, obk[yl] + y0k[...])
        yield
        for it in (0, 1):
            dir1[it].wait_recv()
            mer1[it].wait_recv()
            base = half + it * quar
            out(base, quar, part[did(x, yl, c), pl.ds(base, quar)] + r1k[it, 1] + r1k[it, 2])
            yield

    def entered():
        for r in range(3):
            for dev in (ZP, ZM):
                pl.semaphore_signal(tok.at[r], inc=1, device_id=dev, device_id_type=MESH)
            yield
            pl.semaphore_wait(tok.at[r], 2)
        pl.semaphore_signal(tok.at[3], inc=1, device_id=YH, device_id_type=MESH)
        yield
        pl.semaphore_wait(tok.at[3], 1)

    def flip_w():
        ld_w.wait()
        for g in range(4):

            @pl.loop(0, 4)
            def _(q, g=g):
                at = pl.multiple_of((g * 4 + q) * B, B)
                xw[pl.ds(T, B), pl.ds(at, B)] = xwt[pl.ds(at, B), pl.ds(T, B)].T

            yield
        ld_x.wait()

    def flip_x():
        for g in range(4):

            @pl.loop(0, 4)
            def _(q, g=g):
                at = pl.multiple_of((g * 4 + q) * B, B)
                xwt[pl.ds(at, B), pl.ds(0, T)] = xw[pl.ds(0, T), pl.ds(at, B)].T

            yield

    def mask():
        ld_c.wait()
        slot = T // len_ref.shape[0]
        for s in range(len_ref.shape[0]):
            keep = lax.broadcasted_iota(jnp.int32, (slot, cot.shape[1]), 0) < len_ref[s]
            cur = cot[pl.ds(s * slot, slot)].astype(F32)
            cot[pl.ds(s * slot, slot)] = jnp.where(keep, cur, 0.0).astype(BF)
            yield

    def cols(idx):
        return pl.ds(pl.multiple_of(idx * B, B), B)

    def rotate(r):
        def use(idx):
            s32[...] += nn(xw[:, cols(idx)], r[cols(idx)])

        return use

    s32[...] = jnp.zeros_like(s32)
    ga32[...] = jnp.zeros_like(ga32)
    ring_r = gather_loop(r_all)
    first, hello = gather_dp(rhi, rotate(rhi)), entered()
    advance(first, 1)
    advance(ring_r, 1)
    advance(hello, 1)
    drive((flip_w(), 1))
    advance(first, 1)
    advance(hello, 1)
    advance(first, 1)
    advance(ring_r, 1)
    advance(first, 1)
    advance(hello, 1)
    advance(first, 2)
    advance(hello, 1)
    drive((first, 1))
    drive((hello, 1))
    sq = s32[...]
    sq = sq * sq
    NS = s32.shape[0] // 128
    sums = jnp.sum((sq[:, :128] + sq[:, 128:]).T, axis=0, keepdims=True)
    for g in range(NS):
        stat_mine[pl.ds(g, 1)] = sums[:, g * 128 : (g + 1) * 128]
    for g in range(NS, 8):
        stat_mine[pl.ds(g, 1)] = jnp.zeros((1, 128), F32)
    stats = []
    for d in range(1, 16):
        stats.append(
            send(stat_mine, stat_all.at[d], {"dp": i, "loop": lax.rem(j + d, 16)})
        )
    drive((flip_x(), 1), (mask(), 1))
    for cp in stats:
        cp.wait_recv()
    power = stat_mine[...]
    for d in range(1, 16):
        power = power + stat_all[d]
    limit = CLIP_RATIO * jnp.sqrt(power * inv_width + EPS_POWER)
    for g in range(NS):
        lim = jnp.broadcast_to(limit[g : g + 1, :], (128, 128)).T
        for h in (0, 1):
            v = s32[pl.ds(g * 128, 128), pl.ds(h * 128, 128)]
            v = jnp.minimum(jnp.maximum(v, -lim), lim)
            if g * 128 < T:
                aqt[pl.ds(h * 128, 128), pl.ds(g * 128, 128)] = v.T.astype(BF)
            else:
                at = pl.multiple_of(i * B + (g * 128 - T), 128)
                mqt[pl.ds(at, 128), pl.ds(h * 128, 128)] = v.astype(BF)

    advance(ring_r, 4)

    def back(idx):
        ga32[...] += nn(cot[:, cols(idx)], mqt[cols(idx)])

    drive((gather_dp(mqt, back), 1))
    ga = ga32[...]
    gam[pl.ds(0, T)] = ga.astype(BF)
    gat_all[j] = ga.T.astype(BF)

    def chunk_gm(idx):
        return nn(aqt[...], cot[:, pl.ds(pl.multiple_of(idx * B, B), B)])

    def out_gm(at, n, v):
        gm_all[j, pl.ds(at, n)] = v.astype(BF)
        gout[pl.ds(at, n)] = v

    ring_ga, ring_gm = gather_loop(gat_all), gather_loop(gm_all)
    advance(ring_ga, 1)
    drive((reduce_dp(0, part_a, chunk_gm, out_gm), 3), beside=(ring_ga, 1))
    advance(ring_gm, 1)
    gam[pl.ds(T, B)] = gout[...].T.astype(BF)

    def chunk_g(idx):
        return nn(xwt[pl.ds(pl.multiple_of(idx * B, B), B)], gam[...])

    def out_g(at, n, v):
        gout[pl.ds(at, n)] = v * scale

    rings = chain(ring_ga, ring_gm)
    drive((reduce_dp(1, part_b, chunk_g, out_g), 3), beside=(rings, 1))
    drive((gather_dp(rlo, rotate(rlo)), 1), (rings, 1))
    sh, sl = split(s32[...])
    s_hi[...] = sh
    s_lo[...] = sl
    for cp in sent:
        cp.wait_send()
    sent.clear()

    def chunk_c(idx):
        a, b = gat_all[idx], gm_all[idx]
        return (
            nn(a, s_hi[pl.ds(0, T)])
            + nn(a, s_lo[pl.ds(0, T)])
            + nn(b, s_hi[pl.ds(T, B)])
            + nn(b, s_lo[pl.ds(T, B)])
        )

    def out_c(at, n, v):
        cross[pl.ds(pl.multiple_of(i * B + at, B // 4), n)] = v * scale

    drive((reduce_dp(2, part_a, chunk_c, out_c), 3), beside=(ring_r, 1))

    def correct(idx):
        ah, al = split(r_all[idx])
        bh, bl = split(cross[cols(idx)])
        gout[...] -= nn(ah, bh) + nn(ah, bl) + nn(al, bh)

    last = gather_dp(cross, correct)
    advance(last, 1)
    drive((ring_r, 1))
    drive((last, 1))
    out_ref[...] = gout[...]
    for cp in sent:
        cp.wait_send()


def solution(mesh):
    def on_device(tokens, cotangent, proj_weight, rotation, doc_lengths):
        T, D = tokens.shape
        B = rotation.shape[1]
        n = mesh.shape["dp"]
        hbm = pl.BlockSpec(memory_space=pl.ANY)
        total = T * n
        V = pltpu.VMEM

        def body(*refs):
            kernel(1.0 / D, 1.0 / (float(total) ** 0.5), *refs)

        return pl.pallas_call(
            body,
            out_shape=jax.ShapeDtypeStruct((B, B), F32),
            in_specs=[pl.BlockSpec(memory_space=pltpu.SMEM), hbm, hbm, hbm, hbm],
            out_specs=pl.BlockSpec(memory_space=pltpu.VMEM),
            scratch_shapes=[
                V((T + B, D), BF),
                V((D, T + B), BF),
                V((T, D), BF),
                V((D, B), BF),
                V((D, B), BF),
                V((D, B), BF),
                V((T + B, B), F32),
                V((T + B, B), BF),
                V((T + B, B), BF),
                V((8, 128), F32),
                V((16, 8, 128), F32),
                V((T + B, B), BF),
                V((B, T), BF),
                V((16, B, T), BF),
                V((16, B, B), BF),
                V((16, B, B), F32),
                V((16, B, B), F32),
                V((16, B, B), F32),
                V((3, 8, B, B), F32),
                V((3, 2, 3, B // 2, B), F32),
                V((3, 2, 3, B // 4, B), F32),
                V((3, B // 2, B), F32),
                V((3, 4, B // 2, B), F32),
                V((3, 2, B // 2, B), F32),
                V((B, B), F32),
                V((D, B), F32),
                pltpu.SemaphoreType.DMA((SEMS,)),
                pltpu.SemaphoreType.DMA((SEMS,)),
                pltpu.SemaphoreType.DMA((4,)),
                pltpu.SemaphoreType.REGULAR((4,)),
                V((T, B), F32),
            ],
            compiler_params=pltpu.CompilerParams(
                collective_id=0, has_side_effects=True, vmem_limit_bytes=67000000
            ),
        )(doc_lengths, tokens, cotangent, proj_weight, rotation)

    in_specs = (P("dp", None), P("dp", None), P(None, "dp"), P("dp", "loop"), P("dp"))
    return jax.shard_map(
        on_device, mesh=mesh, in_specs=in_specs, out_specs=P("dp", "loop"), check_vma=False
    )
```

```python
import jax
import jax.numpy as jnp
from jax import lax
from jax.experimental import pallas as pl
from jax.experimental.pallas import tpu as pltpu
from jax.sharding import PartitionSpec as P

MESH = pl.DeviceIdType.MESH
BF = jnp.bfloat16
F32 = jnp.float32
CLIP_RATIO = 2.0
EPS_POWER = 1e-06
SEMS = 256


def nn(a, b):
    return lax.dot_general(a, b, (((1,), (0,)), ((), ())), preferred_element_type=F32)


def split(v):
    hi = v.astype(BF)
    return hi, (v - hi.astype(F32)).astype(BF)


def advance(gen, steps):
    for _ in range(steps):
        if next(gen, StopIteration) is StopIteration:
            return False
    return True


def drive(*main, beside=None):
    live = list(main)
    while live:
        for item in list(live):
            if not advance(*item):
                live.remove(item)
        if beside is not None:
            advance(*beside)


def chain(*gens):
    for g in gens:
        yield from g


def kernel(
    inv_width,
    scale,
    len_ref,
    tok_hbm,
    cot_hbm,
    w_hbm,
    rot_hbm,
    out_ref,
    xw,
    xwt,
    cot,
    rhi,
    rlo,
    mqt,
    s32,
    s_hi,
    s_lo,
    stat_mine,
    stat_all,
    gam,
    aqt,
    gat_all,
    gm_all,
    r_all,
    part_a,
    part_b,
    rc,
    rx0,
    rx1,
    ry0,
    ry1,
    ob,
    gout,
    cross,
    ssem,
    rsem,
    lsem,
    tok,
    ga32,
    lim_all,
):
    i = lax.axis_index("dp")
    j = lax.axis_index("loop")
    x, yl, c = i // 4, (i // 2) % 2, i % 2
    yh, z = j // 8, j % 8
    T = tok_hbm.shape[0]
    B = 256

    def wrap4(v):
        return lax.rem(v + 4, 4)

    def wrap8(v):
        return lax.rem(v + 8, 8)

    xp, xm = wrap4(x + 1), wrap4(x - 1)
    x2 = wrap4(x + 2)
    XP = {"dp": xp * 4 + yl * 2 + c, "loop": j}
    XM = {"dp": xm * 4 + yl * 2 + c, "loop": j}
    YN = {"dp": x * 4 + (1 - yl) * 2 + c, "loop": j}
    CORE = {"dp": x * 4 + yl * 2 + (1 - c), "loop": j}
    zp, zm = wrap8(z + 1), wrap8(z - 1)
    ZP = {"dp": i, "loop": yh * 8 + zp}
    ZM = {"dp": i, "loop": yh * 8 + zm}
    YH = {"dp": i, "loop": (1 - yh) * 8 + z}

    def did(xx, yy, cc):
        return xx * 4 + yy * 2 + cc

    counter = [0]
    sent = []

    def send(src, dst, dev):
        k = counter[0]
        counter[0] += 1
        cp = pltpu.make_async_remote_copy(
            src_ref=src,
            dst_ref=dst,
            send_sem=ssem.at[k],
            recv_sem=rsem.at[k],
            device_id=dev,
            device_id_type=MESH,
        )
        cp.start()
        sent.append(cp)
        return cp

    def send_same(ref, dev):
        return send(ref, ref, dev)

    ld_r = pltpu.make_async_copy(rot_hbm, r_all.at[j], lsem.at[0])
    ld_x = pltpu.make_async_copy(tok_hbm, xw.at[pl.ds(0, T)], lsem.at[1])
    ld_w = pltpu.make_async_copy(w_hbm, xwt.at[:, pl.ds(T, B)], lsem.at[2])
    ld_c = pltpu.make_async_copy(cot_hbm, cot, lsem.at[3])
    ld_r.start()
    ld_w.start()
    ld_x.start()
    ld_c.start()

    barrier = pltpu.get_barrier_semaphore()
    for dev in (XP, XM, YN, CORE, ZP, ZM, YH):
        pl.semaphore_signal(barrier, inc=1, device_id=dev, device_id_type=MESH)
    ld_r.wait()
    rv = r_all[j]
    hv, lv = split(rv)
    own_rows = pl.ds(pl.multiple_of(i * B, B), B)
    rhi[own_rows] = hv
    rlo[own_rows] = lv
    pl.semaphore_wait(barrier, 7)

    def rows(buf, idx, part=None):
        if part is None:
            return buf.at[pl.ds(pl.multiple_of(idx * B, B), B)]
        return buf.at[pl.ds(pl.multiple_of(idx * B + part * (B // 2), B // 2), B // 2)]

    def gather_dp(buf, use):
        left, right, opp = did(xm, yl, c), did(xp, yl, c), did(x2, yl, c)
        ynb = did(x, 1 - yl, c)
        lft2, rgt2, opp2 = did(xm, 1 - yl, c), did(xp, 1 - yl, c), did(x2, 1 - yl, c)
        core = []

        def pair(ref, xx=None, yy=None):
            core.append((send_same(ref, CORE), None if xx is None else did(xx, yy, 1 - c)))

        def meet(n):
            for _ in range(n):
                cp, idx = core.pop(0)
                cp.wait_recv()
                if idx is not None:
                    use(idx)

        a_y0 = send_same(rows(buf, i, 0), YN)
        a_p0 = send_same(rows(buf, i, 0), XP)
        a_m1 = send_same(rows(buf, i, 1), XM)
        a_y1 = send_same(rows(buf, i, 1), YN)
        a_p1 = send_same(rows(buf, i, 1), XP)
        a_m0 = send_same(rows(buf, i, 0), XM)
        pair(rows(buf, i), x, yl)
        yield
        use(i)
        a_p0.wait_recv()
        r_p = send_same(rows(buf, left, 0), XP)
        a_m1.wait_recv()
        r_m = send_same(rows(buf, right, 1), XM)
        yield
        a_y0.wait_recv()
        d_p = send_same(rows(buf, ynb, 0), XP)
        a_y1.wait_recv()
        d_m = send_same(rows(buf, ynb, 1), XM)
        yield
        a_p1.wait_recv()
        y_l = send_same(rows(buf, left, 1), YN)
        pair(rows(buf, left), xm, yl)
        a_m0.wait_recv()
        y_r = send_same(rows(buf, right, 0), YN)
        pair(rows(buf, right), xp, yl)
        pair(rows(buf, ynb), x, 1 - yl)
        use(left)
        yield
        r_p.wait_recv()
        y_a = send_same(rows(buf, opp, 0), YN)
        r_m.wait_recv()
        y_b = send_same(rows(buf, opp, 1), YN)
        pair(rows(buf, opp), x2, yl)
        use(right)
        use(ynb)
        meet(1)
        yield
        use(opp)
        meet(1)
        yield
        d_p.wait_recv()
        y_l.wait_recv()
        pair(rows(buf, lft2), xm, 1 - yl)
        use(lft2)
        yield
        d_m.wait_recv()
        y_r.wait_recv()
        pair(rows(buf, rgt2), xp, 1 - yl)
        use(rgt2)
        meet(2)
        yield
        y_a.wait_recv()
        pair(rows(buf, opp2, 0))
        meet(1)
        yield
        y_b.wait_recv()
        pair(rows(buf, opp2, 1), x2, 1 - yl)
        use(opp2)
        meet(len(core))

    def gather_loop(buf):
        half = B // 2

        def blk(u, zz, part=None):
            ref = buf.at[u * 8 + zz]
            if part is None:
                return ref
            return ref.at[pl.ds(part * half, half)]

        own = blk(yh, z)
        oth = send_same(own, YH)
        wp = {0: send_same(own, ZP)}
        wm = {0: send_same(own, ZM)}
        lanes = (yh, 1 - yh)
        yield
        oth.wait_recv()
        wp[1] = send_same(blk(lanes[1], z), ZP)
        wm[1] = send_same(blk(lanes[1], z), ZM)
        yield
        for d in range(1, 5):
            for ln in (0, 1):
                wp[ln].wait_recv()
                if d < 4:
                    ref = blk(lanes[ln], wrap8(z - d), None if d < 3 else 0)
                    wp[ln] = send_same(ref, ZP)
                yield
                wm[ln].wait_recv()
                if d < 4:
                    ref = blk(lanes[ln], wrap8(z + d), None if d < 3 else 1)
                    wm[ln] = send_same(ref, ZM)
                yield

    def reduce_dp(k, part, chunk, out):
        rck, r0k, r1k, y0k, y1k, obk = (b.at[k] for b in (rc, rx0, rx1, ry0, ry1, ob))
        order = [(2, 0), (2, 1), (3, 0), (1, 1), (1, 0), (3, 1), (0, 0), (0, 1)]
        half, quar = B // 2, B // 4
        pend = []

        def flush(keep):
            while len(pend) > keep:
                pend.pop(0)()

        core = {}
        for d, yy in order:
            xx = wrap4(x + d)
            idx = did(xx, yy, 1 - c)
            part[idx] = chunk(idx)

            def go(idx=idx, d=d, yy=yy, xx=xx):
                core[d, yy] = send(part.at[idx], rck.at[xx * 2 + yy], CORE)

            pend.append(go)
            flush(1)
            yield
        relay, direct, yfirst = {}, {}, {}
        for d, yy in order:
            xx = wrap4(x + d)
            idx = did(xx, yy, c)
            v = chunk(idx)
            flush(0)
            core[d, yy].wait_recv()
            part[idx] = v + rck[xx * 2 + yy]
            sgn = 1 if yy == 0 else -1
            fwd, back = (XP, XM) if sgn == 1 else (XM, XP)
            if d == 2:

                def go(idx=idx, yy=yy, fwd=fwd):
                    relay[yy] = send(part.at[idx, pl.ds(0, half)], r0k.at[yy, 0], fwd)

                pend.append(go)
            elif d == (4 - sgn) % 4:

                def go(idx=idx, yy=yy, back=back):
                    direct[yy] = send(part.at[idx, pl.ds(0, half)], r0k.at[yy, 1], back)

                pend.append(go)
            if yy == 1:

                def go(d=d, xx=xx):
                    yfirst[d] = send(
                        part.at[did(xx, 1 - yl, c), pl.ds(half, half)], y1k.at[xx], YN
                    )

                if d in (2, 0):
                    pend.append(go)
            if (d, yy) == (1, 0) or (d, yy) == (3, 1):

                def go(d=d, xx=xx):
                    yfirst[d] = send(
                        part.at[did(xx, 1 - yl, c), pl.ds(half, half)], y1k.at[xx], YN
                    )

                pend.append(go)
            yield
        flush(0)

        def ring_tail(base, n, buf, item, yy, sgn, mine):
            fwd = XP if sgn == 1 else XM
            nxt = xp if sgn == 1 else xm
            ref = part.at[did(nxt, yy, c), pl.ds(base, n)]
            ref[...] = ref[...] + buf[item, 0]
            return send(ref, buf.at[item, 2], fwd)

        merged = {}
        for yy in (0, 1):
            relay[yy].wait_recv()
            merged[yy] = ring_tail(0, half, r0k, yy, yy, 1 if yy == 0 else -1, None)
            yield
        rel1, dir1, mer1 = {}, {}, {}
        for d in (2, 1, 3, 0):
            xx = wrap4(x + d)
            yfirst[d].wait_recv()
            ref = part.at[did(xx, yl, c), pl.ds(half, half)]
            ref[...] = ref[...] + y1k[xx]
            for it, sgn in ((0, 1), (1, -1)):
                fwd, back = (XP, XM) if sgn == 1 else (XM, XP)
                src = part.at[did(xx, yl, c), pl.ds(half + it * quar, quar)]
                if d == 2:
                    rel1[it] = send(src, r1k.at[it, 0], fwd)
                elif d == (4 - sgn) % 4:
                    dir1[it] = send(src, r1k.at[it, 1], back)
            yield
        for yy in (0, 1):
            direct[yy].wait_recv()
            merged[yy].wait_recv()
            obk[yy] = part[did(x, yy, c), pl.ds(0, half)] + r0k[yy, 1] + r0k[yy, 2]
        ysend = send(obk.at[1 - yl], y0k, YN)
        yield
        for it, sgn in ((0, 1), (1, -1)):
            rel1[it].wait_recv()
            mer1[it] = ring_tail(half + it * quar, quar, r1k, it, yl, sgn, None)
            yield
        ysend.wait_recv()
        out(0, half, obk[yl] + y0k[...])
        yield
        for it in (0, 1):
            dir1[it].wait_recv()
            mer1[it].wait_recv()
            base = half + it * quar
            out(base, quar, part[did(x, yl, c), pl.ds(base, quar)] + r1k[it, 1] + r1k[it, 2])
            yield

    def entered():
        for r in range(3):
            for dev in (ZP, ZM):
                pl.semaphore_signal(tok.at[r], inc=1, device_id=dev, device_id_type=MESH)
            yield
            pl.semaphore_wait(tok.at[r], 2)
        pl.semaphore_signal(tok.at[3], inc=1, device_id=YH, device_id_type=MESH)
        yield
        pl.semaphore_wait(tok.at[3], 1)

    def flip_w():
        ld_w.wait()
        for g in range(4):

            @pl.loop(0, 4)
            def _(q, g=g):
                at = pl.multiple_of((g * 4 + q) * B, B)
                xw[pl.ds(T, B), pl.ds(at, B)] = xwt[pl.ds(at, B), pl.ds(T, B)].T

            yield
        ld_x.wait()

    def flip_x():
        for g in range(4):

            @pl.loop(0, 4)
            def _(q, g=g):
                at = pl.multiple_of((g * 4 + q) * B, B)
                xwt[pl.ds(at, B), pl.ds(0, T)] = xw[pl.ds(0, T), pl.ds(at, B)].T

            yield

    def mask():
        ld_c.wait()
        slot = T // len_ref.shape[0]
        for s in range(len_ref.shape[0]):
            keep = lax.broadcasted_iota(jnp.int32, (slot, cot.shape[1]), 0) < len_ref[s]
            cur = cot[pl.ds(s * slot, slot)].astype(F32)
            cot[pl.ds(s * slot, slot)] = jnp.where(keep, cur, 0.0).astype(BF)
            yield

    def cols(idx):
        return pl.ds(pl.multiple_of(idx * B, B), B)

    def rotate(r):
        def use(idx):
            s32[...] += nn(xw[:, cols(idx)], r[cols(idx)])

        return use

    s32[...] = jnp.zeros_like(s32)
    ga32[...] = jnp.zeros_like(ga32)
    ring_r = gather_loop(r_all)
    first, hello = gather_dp(rhi, rotate(rhi)), entered()
    advance(first, 1)
    advance(ring_r, 1)
    advance(hello, 1)
    drive((flip_w(), 1))
    advance(first, 1)
    advance(hello, 1)
    advance(first, 1)
    advance(ring_r, 1)
    advance(first, 1)
    advance(hello, 1)
    advance(first, 2)
    advance(hello, 1)
    drive((first, 1))
    drive((hello, 1))
    mqt[own_rows] = s32[pl.ds(T, B)].astype(BF)
    queue, limits_here = [], []

    def back(idx):
        if not limits_here:
            queue.append(idx)
            return
        halves = []
        for g in (0, 1):
            lim = lim_all[idx, pl.ds(T // 128 + g, 1)]
            lim = jnp.broadcast_to(lim, (128, 128)).T.astype(BF).astype(F32)
            at = pl.multiple_of(idx * B + g * 128, 128)
            row = [mqt[pl.ds(at, 128), pl.ds(h * 128, 128)].astype(F32) for h in (0, 1)]
            row = [jnp.minimum(jnp.maximum(v, -lim), lim).astype(BF) for v in row]
            halves.append(jnp.concatenate(row, axis=1))
        ga32[...] += nn(cot[:, cols(idx)], jnp.concatenate(halves, axis=0))

    mixing = gather_dp(mqt, back)
    sq = s32[...]
    sq = sq * sq
    NS = s32.shape[0] // 128
    sums = jnp.sum((sq[:, :128] + sq[:, 128:]).T, axis=0, keepdims=True)
    for g in range(NS):
        stat_mine[pl.ds(g, 1)] = sums[:, g * 128 : (g + 1) * 128]
    for g in range(NS, 8):
        stat_mine[pl.ds(g, 1)] = jnp.zeros((1, 128), F32)
    advance(mixing, 1)
    stats = []
    for d in range(1, 16):
        stats.append(
            send(stat_mine, stat_all.at[d], {"dp": i, "loop": lax.rem(j + d, 16)})
        )
    advance(mixing, 2)
    drive((flip_x(), 1), (mask(), 1))
    for cp in stats:
        cp.wait_recv()
    power = stat_mine[...]
    for d in range(1, 16):
        power = power + stat_all[d]
    limit = CLIP_RATIO * jnp.sqrt(power * inv_width + EPS_POWER)
    lim_all[i] = limit
    for g in range(T // 128):
        lim = jnp.broadcast_to(limit[g : g + 1, :], (128, 128)).T
        for h in (0, 1):
            v = s32[pl.ds(g * 128, 128), pl.ds(h * 128, 128)]
            v = jnp.minimum(jnp.maximum(v, -lim), lim)
            aqt[pl.ds(h * 128, 128), pl.ds(g * 128, 128)] = v.T.astype(BF)
    told = []
    for d in range(1, 16):
        dev = {"dp": lax.rem(i + d, 16), "loop": j}
        told.append(send_same(lim_all.at[i], dev))
    advance(mixing, 2)
    advance(ring_r, 4)
    for cp in told:
        cp.wait_recv()
    limits_here.append(True)
    for idx in queue:
        back(idx)
    drive((mixing, 1))
    ga = ga32[...]
    gam[pl.ds(0, T)] = ga.astype(BF)
    gat_all[j] = ga.T.astype(BF)

    def chunk_gm(idx):
        return nn(aqt[...], cot[:, pl.ds(pl.multiple_of(idx * B, B), B)])

    def out_gm(at, n, v):
        gm_all[j, pl.ds(at, n)] = v.astype(BF)
        gout[pl.ds(at, n)] = v

    ring_ga, ring_gm = gather_loop(gat_all), gather_loop(gm_all)
    advance(ring_ga, 1)
    drive((reduce_dp(0, part_a, chunk_gm, out_gm), 3), beside=(ring_ga, 1))
    advance(ring_gm, 1)
    gam[pl.ds(T, B)] = gout[...].T.astype(BF)

    def chunk_g(idx):
        return nn(xwt[pl.ds(pl.multiple_of(idx * B, B), B)], gam[...])

    def out_g(at, n, v):
        gout[pl.ds(at, n)] = v * scale

    rings = chain(ring_ga, ring_gm)
    drive((reduce_dp(1, part_b, chunk_g, out_g), 3), beside=(rings, 1))
    drive((gather_dp(rlo, rotate(rlo)), 1), (rings, 1))
    sh, sl = split(s32[...])
    s_hi[...] = sh
    s_lo[...] = sl
    for cp in sent:
        cp.wait_send()
    sent.clear()

    def chunk_c(idx):
        a, b = gat_all[idx], gm_all[idx]
        return (
            nn(a, s_hi[pl.ds(0, T)])
            + nn(a, s_lo[pl.ds(0, T)])
            + nn(b, s_hi[pl.ds(T, B)])
            + nn(b, s_lo[pl.ds(T, B)])
        )

    def out_c(at, n, v):
        cross[pl.ds(pl.multiple_of(i * B + at, B // 4), n)] = v * scale

    drive((reduce_dp(2, part_a, chunk_c, out_c), 3), beside=(ring_r, 1))

    def correct(idx):
        ah, al = split(r_all[idx])
        bh, bl = split(cross[cols(idx)])
        gout[...] -= nn(ah, bh) + nn(ah, bl) + nn(al, bh)

    last = gather_dp(cross, correct)
    advance(last, 1)
    drive((ring_r, 1))
    drive((last, 1))
    out_ref[...] = gout[...]
    for cp in sent:
        cp.wait_send()


def solution(mesh):
    def on_device(tokens, cotangent, proj_weight, rotation, doc_lengths):
        T, D = tokens.shape
        B = rotation.shape[1]
        n = mesh.shape["dp"]
        hbm = pl.BlockSpec(memory_space=pl.ANY)
        total = T * n
        V = pltpu.VMEM

        def body(*refs):
            kernel(1.0 / D, 1.0 / (float(total) ** 0.5), *refs)

        return pl.pallas_call(
            body,
            out_shape=jax.ShapeDtypeStruct((B, B), F32),
            in_specs=[pl.BlockSpec(memory_space=pltpu.SMEM), hbm, hbm, hbm, hbm],
            out_specs=pl.BlockSpec(memory_space=pltpu.VMEM),
            scratch_shapes=[
                V((T + B, D), BF),
                V((D, T + B), BF),
                V((T, D), BF),
                V((D, B), BF),
                V((D, B), BF),
                V((D, B), BF),
                V((T + B, B), F32),
                V((T + B, B), BF),
                V((T + B, B), BF),
                V((8, 128), F32),
                V((16, 8, 128), F32),
                V((T + B, B), BF),
                V((B, T), BF),
                V((16, B, T), BF),
                V((16, B, B), BF),
                V((16, B, B), F32),
                V((16, B, B), F32),
                V((16, B, B), F32),
                V((3, 8, B, B), F32),
                V((3, 2, 3, B // 2, B), F32),
                V((3, 2, 3, B // 4, B), F32),
                V((3, B // 2, B), F32),
                V((3, 4, B // 2, B), F32),
                V((3, 2, B // 2, B), F32),
                V((B, B), F32),
                V((D, B), F32),
                pltpu.SemaphoreType.DMA((SEMS,)),
                pltpu.SemaphoreType.DMA((SEMS,)),
                pltpu.SemaphoreType.DMA((4,)),
                pltpu.SemaphoreType.REGULAR((4,)),
                V((T, B), F32),
                V((16, 8, 128), F32),
            ],
            compiler_params=pltpu.CompilerParams(
                collective_id=0, has_side_effects=True, vmem_limit_bytes=67000000
            ),
        )(doc_lengths, tokens, cotangent, proj_weight, rotation)

    in_specs = (P("dp", None), P("dp", None), P(None, "dp"), P("dp", "loop"), P("dp"))
    return jax.shard_map(
        on_device, mesh=mesh, in_specs=in_specs, out_specs=P("dp", "loop"), check_vma=False
    )
```

```python
import jax
import jax.numpy as jnp
from jax import lax
from jax.experimental import pallas as pl
from jax.experimental.pallas import tpu as pltpu
from jax.sharding import PartitionSpec as P

MESH = pl.DeviceIdType.MESH
BF = jnp.bfloat16
F32 = jnp.float32
CLIP_RATIO = 2.0
EPS_POWER = 1e-06
SEMS = 256


def nn(a, b):
    return lax.dot_general(a, b, (((1,), (0,)), ((), ())), preferred_element_type=F32)


def split(v):
    hi = v.astype(BF)
    return hi, (v - hi.astype(F32)).astype(BF)


def advance(gen, steps):
    for _ in range(steps):
        if next(gen, StopIteration) is StopIteration:
            return False
    return True


def drive(*main, beside=None):
    live = list(main)
    while live:
        for item in list(live):
            if not advance(*item):
                live.remove(item)
        if beside is not None:
            advance(*beside)


def chain(*gens):
    for g in gens:
        yield from g


def kernel(
    inv_width,
    scale,
    len_ref,
    tok_hbm,
    cot_hbm,
    w_hbm,
    rot_hbm,
    out_ref,
    xw,
    xwt,
    cot,
    rhi,
    rlo,
    mqt,
    s32,
    s_hi,
    s_lo,
    stat_mine,
    stat_all,
    gam,
    aqt,
    gat_all,
    gm_all,
    r_all,
    part_a,
    part_b,
    rc,
    rx0,
    rx1,
    ry0,
    ry1,
    ob,
    gout,
    cross,
    ssem,
    rsem,
    lsem,
    tok,
    ga32,
    lim_all,
):
    i = lax.axis_index("dp")
    j = lax.axis_index("loop")
    x, yl, c = i // 4, (i // 2) % 2, i % 2
    yh, z = j // 8, j % 8
    T = tok_hbm.shape[0]
    B = 256

    def wrap4(v):
        return lax.rem(v + 4, 4)

    def wrap8(v):
        return lax.rem(v + 8, 8)

    xp, xm = wrap4(x + 1), wrap4(x - 1)
    x2 = wrap4(x + 2)
    XP = {"dp": xp * 4 + yl * 2 + c, "loop": j}
    XM = {"dp": xm * 4 + yl * 2 + c, "loop": j}
    YN = {"dp": x * 4 + (1 - yl) * 2 + c, "loop": j}
    CORE = {"dp": x * 4 + yl * 2 + (1 - c), "loop": j}
    zp, zm = wrap8(z + 1), wrap8(z - 1)
    ZP = {"dp": i, "loop": yh * 8 + zp}
    ZM = {"dp": i, "loop": yh * 8 + zm}
    YH = {"dp": i, "loop": (1 - yh) * 8 + z}

    def did(xx, yy, cc):
        return xx * 4 + yy * 2 + cc

    counter = [0]
    sent = []

    def send(src, dst, dev):
        k = counter[0]
        counter[0] += 1
        cp = pltpu.make_async_remote_copy(
            src_ref=src,
            dst_ref=dst,
            send_sem=ssem.at[k],
            recv_sem=rsem.at[k],
            device_id=dev,
            device_id_type=MESH,
        )
        cp.start()
        sent.append(cp)
        return cp

    def send_same(ref, dev):
        return send(ref, ref, dev)

    ld_r = pltpu.make_async_copy(rot_hbm, r_all.at[j], lsem.at[0])
    ld_x = pltpu.make_async_copy(tok_hbm, xw.at[pl.ds(0, T)], lsem.at[1])
    ld_w = pltpu.make_async_copy(w_hbm, xwt.at[:, pl.ds(T, B)], lsem.at[2])
    ld_c = pltpu.make_async_copy(cot_hbm, cot, lsem.at[3])
    ld_r.start()
    ld_w.start()
    ld_x.start()
    ld_c.start()

    barrier = pltpu.get_barrier_semaphore()
    for dev in (XP, XM, YN, CORE, ZP, ZM, YH):
        pl.semaphore_signal(barrier, inc=1, device_id=dev, device_id_type=MESH)
    ld_r.wait()
    rv = r_all[j]
    hv, lv = split(rv)
    own_rows = pl.ds(pl.multiple_of(i * B, B), B)
    rhi[own_rows] = hv
    rlo[own_rows] = lv
    pl.semaphore_wait(barrier, 7)

    def rows(buf, idx, part=None):
        if part is None:
            return buf.at[pl.ds(pl.multiple_of(idx * B, B), B)]
        return buf.at[pl.ds(pl.multiple_of(idx * B + part * (B // 2), B // 2), B // 2)]

    def gather_dp(buf, use):
        left, right, opp = did(xm, yl, c), did(xp, yl, c), did(x2, yl, c)
        ynb = did(x, 1 - yl, c)
        lft2, rgt2, opp2 = did(xm, 1 - yl, c), did(xp, 1 - yl, c), did(x2, 1 - yl, c)
        core = []

        def pair(ref, xx=None, yy=None):
            core.append((send_same(ref, CORE), None if xx is None else did(xx, yy, 1 - c)))

        def meet(n):
            for _ in range(n):
                cp, idx = core.pop(0)
                cp.wait_recv()
                if idx is not None:
                    use(idx)

        a_y0 = send_same(rows(buf, i, 0), YN)
        a_p0 = send_same(rows(buf, i, 0), XP)
        a_m1 = send_same(rows(buf, i, 1), XM)
        a_y1 = send_same(rows(buf, i, 1), YN)
        a_p1 = send_same(rows(buf, i, 1), XP)
        a_m0 = send_same(rows(buf, i, 0), XM)
        pair(rows(buf, i), x, yl)
        yield
        use(i)
        a_p0.wait_recv()
        r_p = send_same(rows(buf, left, 0), XP)
        a_m1.wait_recv()
        r_m = send_same(rows(buf, right, 1), XM)
        yield
        a_y0.wait_recv()
        d_p = send_same(rows(buf, ynb, 0), XP)
        a_y1.wait_recv()
        d_m = send_same(rows(buf, ynb, 1), XM)
        yield
        a_p1.wait_recv()
        y_l = send_same(rows(buf, left, 1), YN)
        pair(rows(buf, left), xm, yl)
        a_m0.wait_recv()
        y_r = send_same(rows(buf, right, 0), YN)
        pair(rows(buf, right), xp, yl)
        pair(rows(buf, ynb), x, 1 - yl)
        use(left)
        yield
        r_p.wait_recv()
        y_a = send_same(rows(buf, opp, 0), YN)
        r_m.wait_recv()
        y_b = send_same(rows(buf, opp, 1), YN)
        pair(rows(buf, opp), x2, yl)
        use(right)
        use(ynb)
        meet(1)
        yield
        use(opp)
        meet(1)
        yield
        d_p.wait_recv()
        y_l.wait_recv()
        pair(rows(buf, lft2), xm, 1 - yl)
        use(lft2)
        yield
        d_m.wait_recv()
        y_r.wait_recv()
        pair(rows(buf, rgt2), xp, 1 - yl)
        use(rgt2)
        meet(2)
        yield
        y_a.wait_recv()
        pair(rows(buf, opp2, 0))
        meet(1)
        yield
        y_b.wait_recv()
        pair(rows(buf, opp2, 1), x2, 1 - yl)
        use(opp2)
        meet(len(core))

    def gather_loop(buf):
        half = B // 2

        def blk(u, zz, part=None):
            ref = buf.at[u * 8 + zz]
            if part is None:
                return ref
            return ref.at[pl.ds(part * half, half)]

        own = blk(yh, z)
        oth = send_same(own, YH)
        wp = {0: send_same(own, ZP)}
        wm = {0: send_same(own, ZM)}
        lanes = (yh, 1 - yh)
        yield
        oth.wait_recv()
        wp[1] = send_same(blk(lanes[1], z), ZP)
        wm[1] = send_same(blk(lanes[1], z), ZM)
        yield
        for d in range(1, 5):
            for ln in (0, 1):
                wp[ln].wait_recv()
                if d < 4:
                    ref = blk(lanes[ln], wrap8(z - d), None if d < 3 else 0)
                    wp[ln] = send_same(ref, ZP)
                yield
                wm[ln].wait_recv()
                if d < 4:
                    ref = blk(lanes[ln], wrap8(z + d), None if d < 3 else 1)
                    wm[ln] = send_same(ref, ZM)
                yield

    def reduce_dp(k, part, chunk, out):
        rck, r0k, r1k, y0k, y1k, obk = (b.at[k] for b in (rc, rx0, rx1, ry0, ry1, ob))
        order = [(2, 0), (2, 1), (3, 0), (1, 1), (1, 0), (3, 1), (0, 0), (0, 1)]
        half, quar = B // 2, B // 4
        pend = []

        def flush(keep):
            while len(pend) > keep:
                pend.pop(0)()

        core = {}
        for d, yy in order:
            xx = wrap4(x + d)
            idx = did(xx, yy, 1 - c)
            part[idx] = chunk(idx)

            def go(idx=idx, d=d, yy=yy, xx=xx):
                core[d, yy] = send(part.at[idx], rck.at[xx * 2 + yy], CORE)

            pend.append(go)
            flush(1)
            yield
        relay, direct, yfirst = {}, {}, {}
        for d, yy in order:
            xx = wrap4(x + d)
            idx = did(xx, yy, c)
            v = chunk(idx)
            flush(0)
            core[d, yy].wait_recv()
            part[idx] = v + rck[xx * 2 + yy]
            sgn = 1 if yy == 0 else -1
            fwd, back = (XP, XM) if sgn == 1 else (XM, XP)
            if d == 2:

                def go(idx=idx, yy=yy, fwd=fwd):
                    relay[yy] = send(part.at[idx, pl.ds(0, half)], r0k.at[yy, 0], fwd)

                pend.append(go)
            elif d == (4 - sgn) % 4:

                def go(idx=idx, yy=yy, back=back):
                    direct[yy] = send(part.at[idx, pl.ds(0, half)], r0k.at[yy, 1], back)

                pend.append(go)
            if yy == 1:

                def go(d=d, xx=xx):
                    yfirst[d] = send(
                        part.at[did(xx, 1 - yl, c), pl.ds(half, half)], y1k.at[xx], YN
                    )

                if d in (2, 0):
                    pend.append(go)
            if (d, yy) == (1, 0) or (d, yy) == (3, 1):

                def go(d=d, xx=xx):
                    yfirst[d] = send(
                        part.at[did(xx, 1 - yl, c), pl.ds(half, half)], y1k.at[xx], YN
                    )

                pend.append(go)
            yield
        flush(0)

        def ring_tail(base, n, buf, item, yy, sgn, mine):
            fwd = XP if sgn == 1 else XM
            nxt = xp if sgn == 1 else xm
            ref = part.at[did(nxt, yy, c), pl.ds(base, n)]
            ref[...] = ref[...] + buf[item, 0]
            return send(ref, buf.at[item, 2], fwd)

        merged = {}
        for yy in (0, 1):
            relay[yy].wait_recv()
            merged[yy] = ring_tail(0, half, r0k, yy, yy, 1 if yy == 0 else -1, None)
            yield
        rel1, dir1, mer1 = {}, {}, {}
        for d in (2, 1, 3, 0):
            xx = wrap4(x + d)
            yfirst[d].wait_recv()
            ref = part.at[did(xx, yl, c), pl.ds(half, half)]
            ref[...] = ref[...] + y1k[xx]
            for it, sgn in ((0, 1), (1, -1)):
                fwd, back = (XP, XM) if sgn == 1 else (XM, XP)
                src = part.at[did(xx, yl, c), pl.ds(half + it * quar, quar)]
                if d == 2:
                    rel1[it] = send(src, r1k.at[it, 0], fwd)
                elif d == (4 - sgn) % 4:
                    dir1[it] = send(src, r1k.at[it, 1], back)
            yield
        for yy in (0, 1):
            direct[yy].wait_recv()
            merged[yy].wait_recv()
            obk[yy] = part[did(x, yy, c), pl.ds(0, half)] + r0k[yy, 1] + r0k[yy, 2]
        ysend = send(obk.at[1 - yl], y0k, YN)
        yield
        for it, sgn in ((0, 1), (1, -1)):
            rel1[it].wait_recv()
            mer1[it] = ring_tail(half + it * quar, quar, r1k, it, yl, sgn, None)
            yield
        ysend.wait_recv()
        out(0, half, obk[yl] + y0k[...])
        yield
        for it in (0, 1):
            dir1[it].wait_recv()
            mer1[it].wait_recv()
            base = half + it * quar
            out(base, quar, part[did(x, yl, c), pl.ds(base, quar)] + r1k[it, 1] + r1k[it, 2])
            yield

    def entered():
        for r in range(3):
            for dev in (ZP, ZM):
                pl.semaphore_signal(tok.at[r], inc=1, device_id=dev, device_id_type=MESH)
            yield
            pl.semaphore_wait(tok.at[r], 2)
        pl.semaphore_signal(tok.at[3], inc=1, device_id=YH, device_id_type=MESH)
        yield
        pl.semaphore_wait(tok.at[3], 1)

    def flip_w():
        ld_w.wait()
        for g in range(4):

            @pl.loop(0, 4)
            def _(q, g=g):
                at = pl.multiple_of((g * 4 + q) * B, B)
                xw[pl.ds(T, B), pl.ds(at, B)] = xwt[pl.ds(at, B), pl.ds(T, B)].T

            yield
        ld_x.wait()

    def flip_x():
        for g in range(4):

            @pl.loop(0, 4)
            def _(q, g=g):
                at = pl.multiple_of((g * 4 + q) * B, B)
                xwt[pl.ds(at, B), pl.ds(0, T)] = xw[pl.ds(0, T), pl.ds(at, B)].T

            yield

    def mask():
        ld_c.wait()
        slot = T // len_ref.shape[0]
        for s in range(len_ref.shape[0]):
            keep = lax.broadcasted_iota(jnp.int32, (slot, cot.shape[1]), 0) < len_ref[s]
            cur = cot[pl.ds(s * slot, slot)].astype(F32)
            cot[pl.ds(s * slot, slot)] = jnp.where(keep, cur, 0.0).astype(BF)
            yield

    def cols(idx):
        return pl.ds(pl.multiple_of(idx * B, B), B)

    def rotate(r):
        def use(idx):
            s32[...] += nn(xw[:, cols(idx)], r[cols(idx)])

        return use

    s32[...] = jnp.zeros_like(s32)
    ga32[...] = jnp.zeros_like(ga32)
    ring_r = gather_loop(r_all)
    first, hello = gather_dp(rhi, rotate(rhi)), entered()
    advance(first, 1)
    advance(ring_r, 1)
    advance(hello, 1)
    drive((flip_w(), 1))
    advance(first, 1)
    advance(hello, 1)
    advance(first, 1)
    advance(ring_r, 1)
    advance(first, 1)
    advance(hello, 1)
    advance(first, 2)
    advance(hello, 1)
    drive((first, 1))
    drive((hello, 1))
    mqt[own_rows] = s32[pl.ds(T, B)].astype(BF)
    queue, limits_here = [], []

    def back(idx):
        if not limits_here:
            queue.append(idx)
            return
        halves = []
        for g in (0, 1):
            lim = lim_all[idx, pl.ds(T // 128 + g, 1)]
            lim = jnp.broadcast_to(lim, (128, 128)).T.astype(BF).astype(F32)
            at = pl.multiple_of(idx * B + g * 128, 128)
            row = [mqt[pl.ds(at, 128), pl.ds(h * 128, 128)].astype(F32) for h in (0, 1)]
            row = [jnp.minimum(jnp.maximum(v, -lim), lim).astype(BF) for v in row]
            halves.append(jnp.concatenate(row, axis=1))
        ga32[...] += nn(cot[:, cols(idx)], jnp.concatenate(halves, axis=0))

    mixing = gather_dp(mqt, back)
    sq = s32[...]
    sq = sq * sq
    NS = s32.shape[0] // 128
    sums = jnp.sum((sq[:, :128] + sq[:, 128:]).T, axis=0, keepdims=True)
    for g in range(NS):
        stat_mine[pl.ds(g, 1)] = sums[:, g * 128 : (g + 1) * 128]
    for g in range(NS, 8):
        stat_mine[pl.ds(g, 1)] = jnp.zeros((1, 128), F32)
    advance(mixing, 1)
    stats = []
    for d in range(1, 16):
        stats.append(
            send(stat_mine, stat_all.at[d], {"dp": i, "loop": lax.rem(j + d, 16)})
        )
    advance(mixing, 2)
    drive((flip_x(), 1), (mask(), 1))
    for cp in stats:
        cp.wait_recv()
    power = stat_mine[...]
    for d in range(1, 16):
        power = power + stat_all[d]
    limit = CLIP_RATIO * jnp.sqrt(power * inv_width + EPS_POWER)
    lim_all[i] = limit
    for g in range(T // 128):
        lim = jnp.broadcast_to(limit[g : g + 1, :], (128, 128)).T
        for h in (0, 1):
            v = s32[pl.ds(g * 128, 128), pl.ds(h * 128, 128)]
            v = jnp.minimum(jnp.maximum(v, -lim), lim)
            aqt[pl.ds(h * 128, 128), pl.ds(g * 128, 128)] = v.T.astype(BF)
    told = []
    for d in range(1, 16):
        dev = {"dp": lax.rem(i + d, 16), "loop": j}
        told.append(send_same(lim_all.at[i], dev))
    advance(mixing, 2)
    advance(ring_r, 4)
    for cp in told:
        cp.wait_recv()
    limits_here.append(True)
    for idx in queue:
        back(idx)
    drive((mixing, 1))
    ga = ga32[...]
    gam[pl.ds(0, T)] = ga.astype(BF)
    gat_all[j] = ga.T.astype(BF)

    def chunk_gm(idx):
        return nn(aqt[...], cot[:, pl.ds(pl.multiple_of(idx * B, B), B)])

    def out_gm(at, n, v):
        gm_all[j, pl.ds(at, n)] = v.astype(BF)
        gout[pl.ds(at, n)] = v

    ring_ga, ring_gm = gather_loop(gat_all), gather_loop(gm_all)
    advance(ring_ga, 1)
    drive((reduce_dp(0, part_a, chunk_gm, out_gm), 3), beside=(ring_ga, 1))
    advance(ring_gm, 1)
    gam[pl.ds(T, B)] = gout[...].T.astype(BF)

    def chunk_g(idx):
        return nn(xwt[pl.ds(pl.multiple_of(idx * B, B), B)], gam[...])

    def out_g(at, n, v):
        gout[pl.ds(at, n)] = v * scale

    rings = chain(ring_ga, ring_gm)
    drive((reduce_dp(1, part_b, chunk_g, out_g), 3), beside=(rings, 1))
    drive((gather_dp(rlo, rotate(rlo)), 1), (rings, 1))
    sh, sl = split(s32[...])
    s_hi[...] = sh
    s_lo[...] = sl
    for cp in sent:
        cp.wait_send()
    sent.clear()

    def chunk_c(idx):
        a, b = gat_all[idx], gm_all[idx]
        return (
            nn(a, s_hi[pl.ds(0, T)])
            + nn(a, s_lo[pl.ds(0, T)])
            + nn(b, s_hi[pl.ds(T, B)])
            + nn(b, s_lo[pl.ds(T, B)])
        )

    def out_c(at, n, v):
        cross[pl.ds(pl.multiple_of(i * B + at, B // 4), n)] = v * scale

    drive((reduce_dp(2, part_a, chunk_c, out_c), 4), beside=(ring_r, 1))

    def correct(idx):
        ah, al = split(r_all[idx])
        bh, bl = split(cross[cols(idx)])
        gout[...] -= nn(ah, bh) + nn(ah, bl) + nn(al, bh)

    last = gather_dp(cross, correct)
    advance(last, 1)
    drive((ring_r, 1))
    drive((last, 1))
    out_ref[...] = gout[...]
    for cp in sent:
        cp.wait_send()


def solution(mesh):
    def on_device(tokens, cotangent, proj_weight, rotation, doc_lengths):
        T, D = tokens.shape
        B = rotation.shape[1]
        n = mesh.shape["dp"]
        hbm = pl.BlockSpec(memory_space=pl.ANY)
        total = T * n
        V = pltpu.VMEM

        def body(*refs):
            kernel(1.0 / D, 1.0 / (float(total) ** 0.5), *refs)

        return pl.pallas_call(
            body,
            out_shape=jax.ShapeDtypeStruct((B, B), F32),
            in_specs=[pl.BlockSpec(memory_space=pltpu.SMEM), hbm, hbm, hbm, hbm],
            out_specs=pl.BlockSpec(memory_space=pltpu.VMEM),
            scratch_shapes=[
                V((T + B, D), BF),
                V((D, T + B), BF),
                V((T, D), BF),
                V((D, B), BF),
                V((D, B), BF),
                V((D, B), BF),
                V((T + B, B), F32),
                V((T + B, B), BF),
                V((T + B, B), BF),
                V((8, 128), F32),
                V((16, 8, 128), F32),
                V((T + B, B), BF),
                V((B, T), BF),
                V((16, B, T), BF),
                V((16, B, B), BF),
                V((16, B, B), F32),
                V((16, B, B), F32),
                V((16, B, B), F32),
                V((3, 8, B, B), F32),
                V((3, 2, 3, B // 2, B), F32),
                V((3, 2, 3, B // 4, B), F32),
                V((3, B // 2, B), F32),
                V((3, 4, B // 2, B), F32),
                V((3, 2, B // 2, B), F32),
                V((B, B), F32),
                V((D, B), F32),
                pltpu.SemaphoreType.DMA((SEMS,)),
                pltpu.SemaphoreType.DMA((SEMS,)),
                pltpu.SemaphoreType.DMA((4,)),
                pltpu.SemaphoreType.REGULAR((4,)),
                V((T, B), F32),
                V((16, 8, 128), F32),
            ],
            compiler_params=pltpu.CompilerParams(
                collective_id=0, has_side_effects=True, vmem_limit_bytes=67000000
            ),
        )(doc_lengths, tokens, cotangent, proj_weight, rotation)

    in_specs = (P("dp", None), P("dp", None), P(None, "dp"), P("dp", "loop"), P("dp"))
    return jax.shard_map(
        on_device, mesh=mesh, in_specs=in_specs, out_specs=P("dp", "loop"), check_vma=False
    )
```
